128 devices in a mesh: lat: 4 (over y_lo, core), lon: 32 (over z, x, y_hi).
Axes of the slice: x: 4, y: 4 (y_hi: 2, y_lo: 2; y = y_hi * 2 + y_lo), z: 4, core: 2. Of those that a mesh axis runs over, the one named last changes fastest.
Arguments:
- observation_residual: bfloat16 [128, 262144], P(None, ('lat', 'lon')), may hold values from -6 to 6
- obs_index: int32 [2, 262144], P(None, ('lat', 'lon')), may hold values from 0 to 8191, as said below
- obs_count: int32 [1, 16384], P(None, ('lat', 'lon')), may hold values from 12 to 16, as said below
- obs_weight: float32 [128], replicated, may hold values from 0.3 to 3
- jacobian: bfloat16 [128, 8, 137], replicated, may hold values from -0.5 to 0.5
- decoder: bfloat16 [137, 128], replicated, may hold values from -0.5 to 0.5
- conv_weight: bfloat16 [4, 3, 128, 128], replicated, may hold values from -0.3125 to 0.3125
- gates: bfloat16 [4, 128, 2048, 512], P(None, None, 'lon', 'lat'), may hold values from 0.049804688 to 1.09375
- encoder: bfloat16 [128, 137], replicated, may hold values from -0.5 to 0.5
Outputs:
- state_grad: float32 [137, 2048, 512], P(None, 'lon', 'lat')
The draws below stay inside these ranges and needn't reach their ends.
Inputs may be any that keep to these rules, and one draw needn't show every extreme that they name: `obs_index`: row 0 is a column within the destination tile, longitude offset * 128 + latitude offset, up to 8191; row 1 is a Jacobian block below 8. `obs_count`: slots of a pair at or after its count are unused. In every draw some tiles receive 16 from every sender.
All inputs are finite; a program needn't handle non-finite values.
Results may differ from the reference program's by a relative error of at most 0.0056.
Values may be sent and summed in bfloat16 or wider, within the bound.
No kernel may reach another device: no remote copies, remote signals or barrier semaphores. Data moves between devices by JAX's collectives and lax.ppermute only.
A program may use at most 128 MiB of HBM per device.

```python
import math
import jax
import jax.numpy as jnp
from jax import lax

C = 128
CH = 128
LEV = 137
NCLASS = 8
LAYERS = 4
TLAT = 128
TLON = 64
SLOT = 16
CELLS = 8192
NLAT = 512
NLON = 2048
NOBS = 262144
N_LAT = 4
N_LON = 32
DEVICES = 128


def draw_obs_count(key, part):
    key_order = jax.random.fold_in(key, 11)
    key_light = jax.random.fold_in(key, 12)
    heavy_count = max(1, DEVICES // 16)
    order = jax.random.permutation(key_order, DEVICES)
    heavy = order < heavy_count
    lowest = SLOT - max(1, SLOT // 4)
    light = jax.random.randint(key_light, (DEVICES, DEVICES), lowest, SLOT + 1)
    counts = jnp.where(heavy[None, :], SLOT, light)
    return counts.reshape(1, DEVICES * DEVICES).astype(jnp.int32)


def draw_obs_index(key, part):
    key_cells = jax.random.fold_in(key, 21)
    key_kinds = jax.random.fold_in(key, 22)
    key_place = jax.random.fold_in(key, 23)
    cells = jax.random.randint(key_cells, (NOBS,), 0, CELLS)
    place = jax.random.randint(key_place, (), 0, NOBS)
    cells = cells.at[place].set(CELLS - 1)
    kinds = jax.random.randint(key_kinds, (NOBS,), 0, NCLASS)
    return jnp.stack([cells, kinds]).astype(jnp.int32)


def block_scale(own_key, dims, pieces, smallest, high):
    loudness = 1.0
    for dim, blocks in pieces:
        draws = jax.random.uniform(jax.random.fold_in(jax.random.fold_in(own_key, 6), dim), (blocks,), jnp.float32, smallest / len(pieces), high / len(pieces))
        loudness = loudness * jnp.repeat(jnp.exp(draws), dims[dim] // blocks).reshape((-1,) + (1,) * (len(dims) - 1 - dim))
    return loudness


def bell_draw(stream_key, dims, scale, most, split=(), kind=jnp.bfloat16):
    drawn = jax.random.normal(stream_key, dims, jnp.float32) * scale
    if len(split) > 0:
        drawn = block_scale(stream_key, dims, split, -0.22, 0.18) * drawn
    return jnp.clip(drawn, min=-most, max=most).astype(kind)


def setup_inputs(seed: int = 0) -> dict:
    splits = jax.random.split(jax.random.key(seed), 10)
    return {
        "observation_residual": bell_draw(splits[0], (CH, NOBS), 1.0, 6.0, ((1, 128),)),
        "obs_index": draw_obs_index(jax.random.fold_in(splits[9], 71), 0),
        "obs_count": draw_obs_count(jax.random.fold_in(splits[9], 71), 0),
        "obs_weight": jnp.clip(jnp.exp(jax.random.uniform(splits[3], (CH,), jnp.float32, math.log(0.3), math.log(3.0))), 0.3, 3.0),
        "jacobian": bell_draw(splits[4], (CH, NCLASS, LEV), CH ** -0.5, 0.5),
        "decoder": bell_draw(splits[5], (LEV, C), C ** -0.5, 0.5),
        "conv_weight": bell_draw(splits[6], (LAYERS, 3, C, C), (3 * C) ** -0.5, 0.3125),
        "gates": jnp.clip(0.049804688 + 1.0439453 * jax.random.uniform(splits[7], (LAYERS, C, NLON, NLAT), jnp.float32) ** block_scale(splits[7], (LAYERS, C, NLON, NLAT), ((2, 32), (3, 4)), -0.2, 0.2), 0.049804688, 1.09375).astype(jnp.bfloat16),
        "encoder": bell_draw(splits[8], (C, LEV), LEV ** -0.5, 0.5),
    }


def rounded(value):
    return lax.optimization_barrier(value.astype(jnp.bfloat16)).astype(jnp.float32)


def reference(observation_residual, obs_index, obs_count, obs_weight, jacobian, decoder, conv_weight, gates, encoder):
    device_count = N_LAT * N_LON
    nobs = observation_residual.shape[1]
    position = jnp.arange(nobs, dtype=jnp.int32)
    pair = position // SLOT
    valid = (position % SLOT) < obs_count[0][pair]
    weighted = rounded(jnp.where(valid[None, :], obs_weight[:, None] * observation_residual.astype(jnp.float32), 0.0))
    kinds = obs_index[1]
    incr = jnp.zeros((LEV, nobs), jnp.float32)
    for kind in range(NCLASS):
        part_incr = jnp.dot(jacobian[:, kind, :].astype(jnp.float32).T, weighted)
        incr = jnp.where(kinds[None, :] == kind, part_incr, incr)
    incr = rounded(incr)
    dest = pair % device_count
    lat_tile = dest // N_LON
    lon_tile = dest % N_LON
    cell = obs_index[0]
    lon_glob = lon_tile * TLON + cell // TLAT
    lat_glob = lat_tile * TLAT + cell % TLAT
    flat = (lon_glob * NLAT + lat_glob).astype(jnp.int32)
    column_grad = jnp.zeros((LEV, NLON * NLAT), jnp.float32).at[:, flat].add(incr)
    hidden = jnp.dot(decoder.astype(jnp.float32).T, rounded(column_grad))
    for layer in reversed(range(LAYERS)):
        field = rounded(hidden).reshape(C, NLON, NLAT)
        back = jnp.zeros((C, NLON * NLAT), jnp.float32)
        for tap in range(3):
            moved = jnp.roll(field, 4 * (tap - 1), axis=1).reshape(C, -1)
            back = back + jnp.dot(conv_weight[layer, tap].astype(jnp.float32).T, moved)
        hidden = hidden + gates[layer].astype(jnp.float32).reshape(C, -1) * back
    state_grad = column_grad + jnp.dot(encoder.astype(jnp.float32).T, rounded(hidden))
    return state_grad.reshape(LEV, NLON, NLAT)
```

```python
import functools

import jax
import jax.numpy as jnp
from jax import lax
from jax.experimental import pallas as pl
from jax.experimental.pallas import tpu as pltpu
from jax.sharding import PartitionSpec as P

F32 = jnp.float32
BF16 = jnp.bfloat16
LANES = 128
CHUNK = 8
DIL = 4
UNUSED = 255.0


def params(mib):
    return pltpu.CompilerParams(vmem_limit_bytes=mib << 20)


def iota(shape, dim):
    return lax.broadcasted_iota(jnp.int32, shape, dim)


def dot(a, b):
    return jnp.dot(a, b, preferred_element_type=F32)


def pack_kernel(resid, index, count, weight, out):
    dests = out.shape[0]
    slots = resid.shape[1]
    per = slots // dests
    weighted = weight[...] * resid[...].astype(F32)
    out[:, 0:per, :] = weighted.astype(BF16).T.reshape(dests, per, LANES)
    spread = (iota((dests, slots), 1) // per == iota((dests, slots), 0)).astype(F32).astype(BF16)
    counts = jnp.broadcast_to(count[...].astype(F32), (8, dests)).astype(BF16)
    used = dot(counts, spread)[0:1]
    cell = index[0:1, :]
    kind = index[1:2, :]
    valid = (iota((1, slots), 1) % per).astype(F32) < used
    low = ((cell >> 7) & (CHUNK - 1)).astype(F32)
    lat = (cell & (LANES - 1)).astype(F32)
    group = jnp.where(valid, (cell >> 10).astype(F32), UNUSED)
    row = iota((LANES, slots), 0) & 63
    meta = jnp.where(
        row == 0, low, jnp.where(row == 1, lat, jnp.where(row == 2, group, kind.astype(F32)))
    )
    meta = meta.astype(BF16).T.reshape(dests, 2, 8, LANES)
    first = meta[:, 0].astype(F32)
    second = meta[:, 1].astype(F32)
    lane = iota((dests, 8, LANES), 2)
    out[:, per : per + 8, :] = jnp.where(lane < 64, first, second).astype(BF16)


def pack(resid, index, count, weight, dests):
    per = resid.shape[1] // dests
    return pl.pallas_call(
        pack_kernel,
        out_shape=jax.ShapeDtypeStruct((dests, per + 8, LANES), BF16),
        compiler_params=params(40),
        name="pack",
    )(resid, index, count, weight)


def gates_kernel(src, out, wide):
    channels, lons, lats = src.shape[1:]

    def widen(c, carry):
        wide[pl.ds(pl.multiple_of(c * lons, lons), lons), :] = src[0, c].astype(F32)
        return carry

    lax.fori_loop(0, channels, widen, 0, unroll=8)

    def gather(lon, carry):
        at = pl.ds(pl.multiple_of(lon * lats, lats), lats)
        for c in range(0, channels, 16):
            a = wide[pl.ds(c * lons + lon, 8, stride=lons), :]
            b = wide[pl.ds((c + 8) * lons + lon, 8, stride=lons), :]
            out[0, c : c + 16, at] = jnp.concatenate([a, b], axis=0).astype(BF16)
        return carry

    lax.fori_loop(0, lons, gather, 0, unroll=2)


def flat_gates(gates):
    layers, channels, lons, lats = gates.shape
    return pl.pallas_call(
        gates_kernel,
        grid=(layers,),
        in_specs=[pl.BlockSpec((1, channels, lons, lats), lambda i: (i, 0, 0, 0))],
        out_specs=pl.BlockSpec((1, channels, lons * lats), lambda i: (i, 0, 0)),
        out_shape=jax.ShapeDtypeStruct((layers, channels, lons * lats), BF16),
        scratch_shapes=[pltpu.VMEM((channels * lons, lats), F32)],
        compiler_params=params(40),
        name="flat_gates",
    )(gates)


def front_kernel(packed, jac, dec, incr_out, key_out, group_out, grad_out, hid_out, lo_out, hi_out):
    senders = packed.shape[0]
    half = senders * 8
    slots = 2 * half
    levels = jac.shape[0]
    kinds = jac.shape[1] // LANES
    x = jnp.concatenate(
        [packed[:, 0:8, :].reshape(half, LANES).T, packed[:, 8:16, :].reshape(half, LANES).T],
        axis=1,
    )
    meta = packed[:, 16:24, :].reshape(half, LANES)
    meta_t = meta.astype(F32).T

    def line(q):
        return jnp.concatenate([meta_t[q : q + 1], meta_t[64 + q : 65 + q]], axis=1)

    def column(q):
        pick = iota((LANES, LANES), 0)
        a = dot(meta, (pick == q).astype(F32).astype(BF16))
        b = dot(meta, (pick == 64 + q).astype(F32).astype(BF16))
        return jnp.concatenate([a, b], axis=0)

    group = line(2)
    kind = line(3)
    group_out[...] = jnp.broadcast_to(group, (8, slots))
    spread = jnp.concatenate(
        [x * (kind == k).astype(F32).astype(BF16) for k in range(kinds)], axis=0
    )
    incr = dot(jac[...], spread).astype(BF16)
    incr_out[...] = incr
    key = column(0) * LANES + column(1) - iota((slots, LANES), 1).astype(F32)
    key_out[...] = key
    onehot = hot(key)
    last = CHUNK - 1
    lhs = jnp.concatenate(
        [incr * (group == g).astype(F32).astype(BF16) for g in (0, last)], axis=0
    )
    grad = dot(lhs, onehot)
    grad_out[...] = grad
    for side in range(2):
        part = grad[side * levels : (side + 1) * levels].astype(BF16)
        hidden = dot(dec[...], part)
        hid_out[side] = hidden
        (lo_out, hi_out)[side][...] = hidden.astype(BF16)


def hot(key):
    return jnp.concatenate(
        [jnp.where(key == float(r * LANES), 1.0, 0.0).astype(BF16) for r in range(CHUNK)], axis=1
    )


def front(packed, jac, dec):
    slots = packed.shape[0] * 16
    levels = jac.shape[0]
    cols = CHUNK * LANES
    sd = jax.ShapeDtypeStruct
    return pl.pallas_call(
        front_kernel,
        out_shape=(
            sd((levels, slots), BF16),
            sd((slots, LANES), F32),
            sd((8, slots), F32),
            sd((2 * levels, cols), F32),
            sd((2, LANES, cols), F32),
            sd((LANES, cols), BF16),
            sd((LANES, cols), BF16),
        ),
        compiler_params=params(56),
        name="front",
    )(packed, jac, dec)


def conv(weight, taps):
    return dot(weight, jnp.concatenate(taps, axis=0))


def inner_layers(hid, ga, gb, gate_a, gate_b, wa, wb, near_out, finish):
    cols = CHUNK * LANES
    step = DIL * LANES
    total = hid.shape[1]
    for i in range(total // cols - 1):
        o = step + i * cols
        at = slice(o, o + cols)
        back = conv(wa[...], [ga[:, o + d : o + d + cols] for d in (step, 0, -step)])
        new = hid[:, at] + gate_a[0, :, at].astype(F32) * back
        hid[:, at] = new
        gb[:, at] = new.astype(BF16)
    near_out[0] = hid[:, step : step + cols]
    near_out[1] = hid[:, total - step - cols : total - step]
    for i in range(1, total // cols - 1):
        o = i * cols
        at = slice(o, o + cols)
        back = conv(wb[...], [gb[:, o + d : o + d + cols] for d in (step, 0, -step)])
        finish(i, hid[:, at] + gate_b[0, :, at].astype(F32) * back)


def mid_kernel(
    incr, key, group, hid_edge, g_lo, g_hi, dec, gate_a, gate_b, wa, wb,
    grad_out, hid_out, near_out, hid, ga, gb, lhs, onehot,
):
    cols = CHUNK * LANES
    levels = incr.shape[0]
    total = hid.shape[1]
    inner = total // cols - 2
    onehot[...] = hot(key[...])
    for g in range(inner):
        mask = (group[0:1, :] == float(g + 1)).astype(F32).astype(BF16)
        lhs[g * levels : (g + 1) * levels, :] = incr[...] * mask
    hid[:, 0:cols] = hid_edge[0]
    hid[:, total - cols : total] = hid_edge[1]
    ga[:, 0:cols] = g_lo[...]
    ga[:, total - cols : total] = g_hi[...]
    for n in range(0, cols, 256):
        grad_out[:, n : n + 256] = dot(lhs[...], onehot[:, n : n + 256])
    for g in range(inner):
        at = slice((g + 1) * cols, (g + 2) * cols)
        new = dot(dec[...], grad_out[g * levels : (g + 1) * levels, :].astype(BF16))
        hid[:, at] = new
        ga[:, at] = new.astype(BF16)

    def finish(i, value):
        hid_out[:, (i - 1) * cols : i * cols] = value

    inner_layers(hid, ga, gb, gate_a, gate_b, wa, wb, near_out, finish)


def whole(shape):
    return pl.BlockSpec(shape, lambda i: (0,) * len(shape))


def mid(incr, key, group, hid_edge, g_lo, g_hi, dec, gates, layer, wa, wb):
    levels, slots = incr.shape
    _, channels, total = gates.shape
    cols = CHUNK * LANES
    inner = total // cols - 2
    sd = jax.ShapeDtypeStruct
    outs = (
        sd((inner * levels, cols), F32),
        sd((channels, inner * cols), F32),
        sd((2, channels, cols), F32),
    )
    return pl.pallas_call(
        mid_kernel,
        grid=(1,),
        in_specs=[
            whole(incr.shape),
            whole(key.shape),
            whole(group.shape),
            whole(hid_edge.shape),
            whole(g_lo.shape),
            whole(g_hi.shape),
            whole(dec.shape),
            pl.BlockSpec((1, channels, total), lambda i: (layer, 0, 0)),
            pl.BlockSpec((1, channels, total), lambda i: (layer - 1, 0, 0)),
            whole(wa.shape),
            whole(wb.shape),
        ],
        out_specs=tuple(whole(o.shape) for o in outs),
        out_shape=outs,
        scratch_shapes=[
            pltpu.VMEM((channels, total), F32),
            pltpu.VMEM((channels, total), BF16),
            pltpu.VMEM((channels, total), BF16),
            pltpu.VMEM((inner * levels, slots), BF16),
            pltpu.VMEM((slots, cols), BF16),
        ],
        compiler_params=params(58),
        name="mid",
    )(incr, key, group, hid_edge, g_lo, g_hi, dec, gates, gates, wa, wb)


def emit(enc, grad, value, tile):
    full = grad + dot(enc, value.astype(BF16))
    for r in range(CHUNK):
        for l in range(0, full.shape[0], 8):
            tile[pl.ds(l * CHUNK + r, 8, stride=CHUNK), :] = full[
                l : l + 8, r * LANES : (r + 1) * LANES
            ]


def send_tile(tile, out, chunk, sem):
    levels = out.shape[0]
    src = tile.reshape(tile.shape[0] // CHUNK, CHUNK, LANES)
    return pltpu.make_async_copy(
        src.at[0:levels], out.at[:, CHUNK * chunk : CHUNK * (chunk + 1), :], sem
    )


def last_kernel(
    hid_in, hid_edge, g_lo, g_hi, grad, enc, gate_a, gate_b, wa, wb,
    out, near_out, hid, ga, gb, tiles, sems,
):
    cols = CHUNK * LANES
    total = hid.shape[1]
    levels = enc.shape[0]
    hid[:, 0:cols] = hid_edge[0]
    hid[:, total - cols : total] = hid_edge[1]
    hid[:, cols : total - cols] = hid_in[...]
    ga[:, 0:cols] = g_lo[...]
    ga[:, total - cols : total] = g_hi[...]
    ga[:, cols : total - cols] = hid_in[...].astype(BF16)
    copies = []

    def finish(i, value):
        slot = (i - 1) % 2
        if i > 2:
            copies[i - 3].wait()
        emit(enc[...], grad[(i - 1) * levels : i * levels, :], value, tiles.at[slot])
        copy = send_tile(tiles.at[slot], out, i, sems.at[slot])
        copy.start()
        copies.append(copy)

    inner_layers(hid, ga, gb, gate_a, gate_b, wa, wb, near_out, finish)
    copies[-2].wait()
    copies[-1].wait()


def last(hid_in, hid_edge, g_lo, g_hi, grad, enc, gates, layer, wa, wb, out_shape):
    _, channels, total = gates.shape
    cols = CHUNK * LANES
    levels = enc.shape[0]
    sd = jax.ShapeDtypeStruct
    near = sd((2, channels, cols), F32)
    return pl.pallas_call(
        last_kernel,
        grid=(1,),
        in_specs=[
            whole(hid_in.shape),
            whole(hid_edge.shape),
            whole(g_lo.shape),
            whole(g_hi.shape),
            whole(grad.shape),
            whole(enc.shape),
            pl.BlockSpec((1, channels, total), lambda i: (layer, 0, 0)),
            pl.BlockSpec((1, channels, total), lambda i: (layer - 1, 0, 0)),
            whole(wa.shape),
            whole(wb.shape),
        ],
        out_specs=(pl.BlockSpec(memory_space=pl.ANY), whole(near.shape)),
        out_shape=(sd(out_shape, F32), near),
        scratch_shapes=[
            pltpu.VMEM((channels, total), F32),
            pltpu.VMEM((channels, total), BF16),
            pltpu.VMEM((channels, total), BF16),
            pltpu.VMEM((2, levels * CHUNK, LANES), F32),
            pltpu.SemaphoreType.DMA((2,)),
        ],
        compiler_params=params(58),
        name="last",
    )(hid_in, hid_edge, g_lo, g_hi, grad, enc, gates, gates, wa, wb)


def edge_values(hid, g_lo, g_hi, halo_lo, halo_hi, near, a_lo, a_hi, ah_lo, ah_hi, b_lo, b_hi, wa, wb):
    cols = CHUNK * LANES
    step = DIL * LANES
    result = []
    for side in range(2):
        if side == 0:
            field = jnp.concatenate([halo_lo[...], g_lo[...]], axis=1)
            old = jnp.concatenate([halo_lo[:, step:].astype(F32), hid[0, :, :step]], axis=1)
            gate = jnp.concatenate([ah_lo[0], a_lo[0, :, :step]], axis=1)
        else:
            field = jnp.concatenate([g_hi[...], halo_hi[...]], axis=1)
            old = jnp.concatenate([hid[1, :, step:], halo_hi[:, :step].astype(F32)], axis=1)
            gate = jnp.concatenate([a_hi[0, :, step:], ah_hi[0]], axis=1)
        back = conv(wa[...], [field[:, d : d + cols] for d in (2 * step, step, 0)])
        new = old + gate.astype(F32) * back
        pieces = (new, near[0]) if side == 0 else (near[1], new)
        joined = jnp.concatenate(pieces, axis=1)
        field = joined.astype(BF16)
        back = conv(wb[...], [field[:, d : d + cols] for d in (2 * step, step, 0)])
        gate = (b_lo, b_hi)[side][0]
        result.append(joined[:, step : step + cols] + gate.astype(F32) * back)
    return result


def edge_kernel(*refs):
    ins, (hid_out, lo_out, hi_out) = refs[:14], refs[14:]
    lo, hi = edge_values(*ins)
    hid_out[0] = lo
    hid_out[1] = hi
    lo_out[...] = lo.astype(BF16)
    hi_out[...] = hi.astype(BF16)


def edge_last_kernel(*refs):
    ins, (grad, enc, _), (out, tiles, sems) = refs[:14], refs[14:17], refs[17:]
    levels = enc.shape[0]
    values = edge_values(*ins)
    chunks = out.shape[1] // CHUNK
    copies = []
    for side in range(2):
        part = grad[side * levels : (side + 1) * levels, :]
        emit(enc[...], part, values[side], tiles.at[side])
        copy = send_tile(tiles.at[side], out, side * (chunks - 1), sems.at[side])
        copy.start()
        copies.append(copy)
    for copy in copies:
        copy.wait()


def edge_call(hid, g_lo, g_hi, halo_lo, halo_hi, near, gates, layer, ah_lo, ah_hi, which, wa, wb, tail=None):
    _, channels, total = gates.shape
    cols = CHUNK * LANES
    step = DIL * LANES
    end = total // cols - 1
    sd = jax.ShapeDtypeStruct

    def gate_at(k, c):
        return pl.BlockSpec((1, channels, cols), lambda i: (k, 0, c))

    halo_at = pl.BlockSpec((1, channels, step), lambda i: (which, 0, 0))
    specs = [
        whole(hid.shape),
        whole(g_lo.shape),
        whole(g_hi.shape),
        whole(halo_lo.shape),
        whole(halo_hi.shape),
        whole(near.shape),
        gate_at(layer, 0),
        gate_at(layer, end),
        halo_at,
        halo_at,
        gate_at(layer - 1, 0),
        gate_at(layer - 1, end),
        whole(wa.shape),
        whole(wb.shape),
    ]
    args = [hid, g_lo, g_hi, halo_lo, halo_hi, near, gates, gates, ah_lo, ah_hi, gates, gates, wa, wb]
    if tail is None:
        outs = (sd(hid.shape, F32), sd(g_lo.shape, BF16), sd(g_hi.shape, BF16))
        return pl.pallas_call(
            edge_kernel,
            grid=(1,),
            in_specs=specs,
            out_specs=tuple(whole(o.shape) for o in outs),
            out_shape=outs,
            compiler_params=params(40),
            name="edge",
        )(*args)
    grad, enc, state = tail
    return pl.pallas_call(
        edge_last_kernel,
        grid=(1,),
        in_specs=specs + [whole(grad.shape), whole(enc.shape), pl.BlockSpec(memory_space=pl.ANY)],
        out_specs=pl.BlockSpec(memory_space=pl.ANY),
        out_shape=sd(state.shape, F32),
        scratch_shapes=[
            pltpu.VMEM((2, enc.shape[0] * CHUNK, LANES), F32),
            pltpu.SemaphoreType.DMA((2,)),
        ],
        input_output_aliases={len(specs) + 2: 0},
        compiler_params=params(40),
        name="edge_last",
    )(*args, grad, enc, state)


def halos(lo, hi):
    count = lax.axis_size("lon")
    up = [(i, (i + 1) % count) for i in range(count)]
    down = [(b, a) for a, b in up]
    return lax.ppermute(hi, "lon", up), lax.ppermute(lo, "lon", down)


def per_device(resid, index, count, weight, jacobian, decoder, conv_weight, gates, encoder):
    dests = lax.axis_size("lat") * lax.axis_size("lon")
    channels, kinds, levels = jacobian.shape
    pad = -levels % 16
    packed = pack(resid, index, count, weight.reshape(-1, 1), dests)
    packed = lax.all_to_all(packed, ("lat", "lon"), split_axis=0, concat_axis=0, tiled=True)
    flat = flat_gates(gates)
    step = DIL * LANES
    gate_lo = jnp.stack([flat[1, :, :step], flat[3, :, :step]])
    gate_hi = jnp.stack([flat[1, :, -step:], flat[3, :, -step:]])
    gh_lo, gh_hi = halos(gate_lo, gate_hi)
    jac = jnp.pad(jacobian.transpose(2, 1, 0).reshape(levels, kinds * channels), ((0, pad), (0, 0)))
    dec = jnp.pad(decoder.T, ((0, 0), (0, pad)))
    enc = jnp.pad(encoder.T, ((0, pad), (0, 0)))
    layers = conv_weight.shape[0]
    w = conv_weight.reshape(layers, -1, channels).transpose(0, 2, 1)

    incr, key, group, grad_e, hid_e, g_lo, g_hi = front(packed, jac, dec)
    halo_lo, halo_hi = halos(g_lo, g_hi)
    grad_i, hid_i, near = mid(incr, key, group, hid_e, g_lo, g_hi, dec, flat, 3, w[3], w[2])
    hid_e, g_lo, g_hi = edge_call(
        hid_e, g_lo, g_hi, halo_lo, halo_hi, near, flat, 3, gh_lo, gh_hi, 1, w[3], w[2]
    )
    halo_lo, halo_hi = halos(g_lo, g_hi)
    out_shape = (levels,) + gates.shape[2:]
    state, near = last(hid_i, hid_e, g_lo, g_hi, grad_i, enc, flat, 1, w[1], w[0], out_shape)
    return edge_call(
        hid_e, g_lo, g_hi, halo_lo, halo_hi, near, flat, 1, gh_lo, gh_hi, 0, w[1], w[0],
        tail=(grad_e, enc, state),
    )


def solution(mesh):
    return jax.shard_map(
        per_device,
        mesh=mesh,
        in_specs=(
            P(None, ("lat", "lon")),
            P(None, ("lat", "lon")),
            P(None, ("lat", "lon")),
            P(),
            P(),
            P(),
            P(),
            P(None, None, "lon", "lat"),
            P(),
        ),
        out_specs=P(None, "lon", "lat"),
        check_vma=False,
    )
```

```python
import functools

import jax
import jax.numpy as jnp
from jax import lax
from jax.experimental import pallas as pl
from jax.experimental.pallas import tpu as pltpu
from jax.sharding import PartitionSpec as P

F32 = jnp.float32
BF16 = jnp.bfloat16
LANES = 128
CHUNK = 8
DIL = 4
UNUSED = 255.0


def params(mib):
    return pltpu.CompilerParams(vmem_limit_bytes=mib << 20)


def iota(shape, dim):
    return lax.broadcasted_iota(jnp.int32, shape, dim)


def dot(a, b):
    return jnp.dot(a, b, preferred_element_type=F32)


def pack_kernel(resid_hbm, index_hbm, count_hbm, weight_hbm, out_hbm, resid, index, count, weight, out, in_sems, out_sems):
    parts, dests = out.shape[:2]
    slots = resid.shape[2]
    per = slots // dests
    small = [
        pltpu.make_async_copy(index_hbm, index, in_sems.at[parts]),
        pltpu.make_async_copy(count_hbm, count, in_sems.at[parts + 1]),
        pltpu.make_async_copy(weight_hbm, weight, in_sems.at[parts + 2]),
    ]
    for copy in small:
        copy.start()
    large = []
    for p in range(parts):
        src = resid_hbm.at[:, p * slots : (p + 1) * slots]
        large.append(pltpu.make_async_copy(src, resid.at[p], in_sems.at[p]))
        large[-1].start()
    for copy in small:
        copy.wait()
    scale = jnp.broadcast_to(weight[...], (LANES, LANES)).T
    scale = jnp.concatenate([scale] * (slots // LANES), axis=1)
    total = dests * parts
    counts = jnp.broadcast_to(count[...].astype(F32), (8, total)).astype(BF16)
    row = iota((LANES, slots), 0) & 63
    lane = iota((dests, 8, LANES), 2)
    sends = []
    for p in range(parts):
        at = slice(p * slots, (p + 1) * slots)
        spread = iota((total, slots), 1) // per + p * dests == iota((total, slots), 0)
        used = dot(counts, spread.astype(F32).astype(BF16))[0:1]
        cell = index[0:1, at]
        kind = index[1:2, at].astype(F32)
        valid = (iota((1, slots), 1) % per).astype(F32) < used
        low = ((cell >> 7) & (CHUNK - 1)).astype(F32)
        lat = (cell & (LANES - 1)).astype(F32)
        group = jnp.where(valid, (cell >> 10).astype(F32), UNUSED)
        meta = jnp.where(row == 0, low, jnp.where(row == 1, lat, jnp.where(row == 2, group, kind)))
        meta = meta.astype(BF16).T.reshape(dests, 2, 8, LANES)
        first = meta[:, 0].astype(F32)
        second = meta[:, 1].astype(F32)
        out[p, :, per : per + 8, :] = jnp.where(lane < 64, first, second).astype(BF16)
        large[p].wait()
        weighted = scale * resid[p].astype(F32)
        out[p, :, 0:per, :] = weighted.astype(BF16).T.reshape(dests, per, LANES)
        dst = out_hbm.at[p * dests : (p + 1) * dests]
        sends.append(pltpu.make_async_copy(out.at[p], dst, out_sems.at[p]))
        sends[-1].start()
    for copy in sends:
        copy.wait()


HBM = pl.BlockSpec(memory_space=pltpu.HBM)
VMEM = pl.BlockSpec(memory_space=pltpu.VMEM)
ANY = pl.BlockSpec(memory_space=pl.ANY)


def pack(resid, index, count, weight, dests):
    channels, slots = resid.shape
    per = slots // dests
    parts = 4
    return pl.pallas_call(
        pack_kernel,
        in_specs=[HBM] * 4,
        out_specs=HBM,
        out_shape=jax.ShapeDtypeStruct((dests, per + 8, LANES), BF16),
        scratch_shapes=[
            pltpu.VMEM((parts, channels, slots // parts), BF16),
            pltpu.VMEM(index.shape, jnp.int32),
            pltpu.VMEM(count.shape, jnp.int32),
            pltpu.VMEM(weight.shape, F32),
            pltpu.VMEM((parts, dests // parts, per + 8, LANES), BF16),
            pltpu.SemaphoreType.DMA((parts + 3,)),
            pltpu.SemaphoreType.DMA((parts,)),
        ],
        compiler_params=params(63),
        name="pack",
    )(resid, index, count, weight)


def by_channel(wide, lon, pitch, c):
    a = wide[pl.ds(c * pitch + lon, 8, stride=pitch), :]
    b = wide[pl.ds((c + 8) * pitch + lon, 8, stride=pitch), :]
    return jnp.concatenate([a, b], axis=0).astype(BF16)


def flatten(src, order, outs, buf, wide, sems):
    channels, lons, lats = src.shape[1:]
    pitch = wide.shape[0] // channels
    copies = [
        pltpu.make_async_copy(src.at[k], buf.at[i], sems.at[i]) for i, k in enumerate(order)
    ]
    for copy in copies:
        copy.start()
    for i, out in enumerate(outs):
        copies[i].wait()

        def widen(c, carry):
            wide[pl.ds(pl.multiple_of(c * pitch, 8), lons), :] = buf[i, c].astype(F32)
            return carry

        lax.fori_loop(0, channels, widen, 0, unroll=8)

        def gather(lon, carry):
            at = pl.ds(pl.multiple_of(lon * lats, lats), lats)
            for c in range(0, channels, 16):
                out[c : c + 16, at] = by_channel(wide, lon, pitch, c)
            return carry

        lax.fori_loop(0, lons, gather, 0, unroll=4)


def gates_scratch(gates):
    layers, channels, lons, lats = gates.shape
    return [
        pltpu.VMEM((2, channels, lons, lats), BF16),
        pltpu.VMEM((channels * (lons + 8), lats), F32),
        pltpu.SemaphoreType.DMA((2,)),
    ]


def prepare_kernel(src, jac, dec, enc, conv_w, f3, f2, jac_out, dec_out, enc_out, w_out, buf, wide, sems, rows, tall):
    levels, kinds = jac.shape[:2]
    padded = enc_out.shape[0]
    rows[...] = jnp.zeros_like(rows)
    rows[0 : levels * kinds, :] = jac[...].astype(F32).reshape(levels * kinds, LANES)
    for k in range(kinds):
        for l in range(0, padded, 16):
            jac_out[l : l + 16, k * LANES : (k + 1) * LANES] = by_channel(rows, k, kinds, l)
    tall[...] = jnp.zeros_like(tall)
    tall[0:levels, :] = enc[...].astype(F32)
    enc_out[...] = tall[0:padded, :].astype(BF16)
    tall[0:levels, :] = dec[...].astype(F32)
    dec_out[...] = tall[...].T[:, 0:padded].astype(BF16)
    for layer in range(conv_w.shape[0]):
        w_out[layer] = conv_w[layer].T
    flatten(src, (3, 2), (f3, f2), buf, wide, sems)


def prepare(gates, jacobian, decoder, encoder, conv_weight):
    layers, channels, lons, lats = gates.shape
    kinds, levels = jacobian.shape[1:]
    padded = levels + -levels % 16
    conv_w = conv_weight.reshape(layers, -1, channels)
    sd = jax.ShapeDtypeStruct
    flat = sd((channels, lons * lats), BF16)
    return pl.pallas_call(
        prepare_kernel,
        in_specs=[HBM] + [VMEM] * 4,
        out_specs=(VMEM,) * 6,
        out_shape=(
            flat,
            flat,
            sd((padded, kinds * channels), BF16),
            sd((channels, padded), BF16),
            sd((padded, channels), BF16),
            sd((layers, channels, conv_w.shape[1]), BF16),
        ),
        scratch_shapes=gates_scratch(gates)
        + [pltpu.VMEM((padded * kinds, channels), F32), pltpu.VMEM((256, channels), F32)],
        compiler_params=params(52),
        name="prepare",
    )(gates, jacobian.transpose(2, 1, 0), decoder, encoder.T, conv_w)


def later_gates_kernel(src, after, f1, f0, buf, wide, sems):
    del after
    flatten(src, (1, 0), (f1, f0), buf, wide, sems)


def later_gates(gates, after):
    layers, channels, lons, lats = gates.shape
    flat = jax.ShapeDtypeStruct((channels, lons * lats), BF16)
    return pl.pallas_call(
        later_gates_kernel,
        in_specs=[HBM, ANY],
        out_specs=(VMEM,) * 2,
        out_shape=(flat,) * 2,
        scratch_shapes=gates_scratch(gates),
        compiler_params=params(46),
        name="later_gates",
    )(gates, after)


def gate_edges_kernel(src, lo, hi, buf, wide, sems):
    channels, lons, lats = src.shape[1:]
    copies = []
    for k in range(2):
        for side in range(2):
            at = side * (lons - CHUNK)
            part = src.at[2 * k + 1, :, at : at + CHUNK, :]
            copies.append(pltpu.make_async_copy(part, buf.at[k, side], sems.at[k, side]))
            copies[-1].start()
    for k in range(2):
        for side, out in enumerate((lo, hi)):
            copies[2 * k + side].wait()
            wide[k, side] = buf[k, side].astype(F32).reshape(channels * CHUNK, lats)
            for r in range(DIL):
                for c in range(0, channels, 16):
                    value = by_channel(wide.at[k, side], side * DIL + r, CHUNK, c)
                    out[k, c : c + 16, r * lats : (r + 1) * lats] = value


def gate_edges(gates):
    layers, channels, lons, lats = gates.shape
    send = jax.ShapeDtypeStruct((2, channels, DIL * lats), BF16)
    return pl.pallas_call(
        gate_edges_kernel,
        in_specs=[HBM],
        out_specs=(VMEM,) * 2,
        out_shape=(send,) * 2,
        scratch_shapes=[
            pltpu.VMEM((2, 2, channels, CHUNK, lats), BF16),
            pltpu.VMEM((2, 2, channels * CHUNK, lats), F32),
            pltpu.SemaphoreType.DMA((2, 2)),
        ],
        compiler_params=params(58),
        name="gate_edges",
    )(gates)


def front_kernel(packed, jac, dec, incr_out, key_out, group_out, grad_out, hid_out, lo_out, hi_out):
    senders = packed.shape[0]
    half = senders * 8
    slots = 2 * half
    levels = jac.shape[0]
    kinds = jac.shape[1] // LANES
    x = jnp.concatenate(
        [packed[:, 0:8, :].reshape(half, LANES).T, packed[:, 8:16, :].reshape(half, LANES).T],
        axis=1,
    )
    meta = packed[:, 16:24, :].reshape(half, LANES)
    meta_t = meta.astype(F32).T

    def line(q):
        return jnp.concatenate([meta_t[q : q + 1], meta_t[64 + q : 65 + q]], axis=1)

    def column(q):
        pick = iota((LANES, LANES), 0)
        a = dot(meta, (pick == q).astype(F32).astype(BF16))
        b = dot(meta, (pick == 64 + q).astype(F32).astype(BF16))
        return jnp.concatenate([a, b], axis=0)

    group = line(2)
    kind = line(3)
    group_out[...] = jnp.broadcast_to(group, (8, slots))
    spread = jnp.concatenate(
        [x * (kind == k).astype(F32).astype(BF16) for k in range(kinds)], axis=0
    )
    incr = dot(jac[...], spread).astype(BF16)
    incr_out[...] = incr
    key = column(0) * LANES + column(1) - iota((slots, LANES), 1).astype(F32)
    key_out[...] = key
    onehot = hot(key)
    last = CHUNK - 1
    lhs = jnp.concatenate(
        [incr * (group == g).astype(F32).astype(BF16) for g in (0, last)], axis=0
    )
    grad = dot(lhs, onehot)
    grad_out[...] = grad
    for side in range(2):
        part = grad[side * levels : (side + 1) * levels].astype(BF16)
        hidden = dot(dec[...], part)
        hid_out[side] = hidden
        (lo_out, hi_out)[side][...] = hidden.astype(BF16)


def hot(key):
    return jnp.concatenate(
        [jnp.where(key == float(r * LANES), 1.0, 0.0).astype(BF16) for r in range(CHUNK)], axis=1
    )


def front(packed, jac, dec):
    slots = packed.shape[0] * 16
    levels = jac.shape[0]
    cols = CHUNK * LANES
    sd = jax.ShapeDtypeStruct
    return pl.pallas_call(
        front_kernel,
        in_specs=[VMEM] * 3,
        out_specs=(VMEM,) * 7,
        out_shape=(
            sd((levels, slots), BF16),
            sd((slots, LANES), F32),
            sd((8, slots), F32),
            sd((2 * levels, cols), F32),
            sd((2, LANES, cols), F32),
            sd((LANES, cols), BF16),
            sd((LANES, cols), BF16),
        ),
        compiler_params=params(28),
        name="front",
    )(packed, jac, dec)


def conv(weight, taps):
    return dot(weight[...], jnp.concatenate(taps, axis=0))


def inner_layers(hid, ga, gb, gate_a, gate_b, wa, wb, near_out, finish):
    cols = CHUNK * LANES
    step = DIL * LANES
    total = hid.shape[1]
    for i in range(total // cols - 1):
        o = step + i * cols
        at = slice(o, o + cols)
        back = conv(wa, [ga[:, o + d : o + d + cols] for d in (step, 0, -step)])
        new = hid[:, at] + gate_a[:, at].astype(F32) * back
        hid[:, at] = new
        gb[:, at] = new.astype(BF16)
    near_out[0] = hid[:, step : step + cols]
    near_out[1] = hid[:, total - step - cols : total - step]
    for i in range(1, total // cols - 1):
        o = i * cols
        at = slice(o, o + cols)
        back = conv(wb, [gb[:, o + d : o + d + cols] for d in (step, 0, -step)])
        finish(i, hid[:, at] + gate_b[:, at].astype(F32) * back)


def mid_kernel(
    incr, key, group, hid_edge, g_lo, g_hi, dec, gate_a, gate_b, w,
    grad_out, hid_out, near_out, hid, ga, gb, lhs, onehot,
):
    cols = CHUNK * LANES
    levels = incr.shape[0]
    total = hid.shape[1]
    inner = total // cols - 2
    onehot[...] = hot(key[...])
    for g in range(inner):
        mask = (group[0:1, :] == float(g + 1)).astype(F32).astype(BF16)
        lhs[g * levels : (g + 1) * levels, :] = incr[...] * mask
    hid[:, 0:cols] = hid_edge[0]
    hid[:, total - cols : total] = hid_edge[1]
    ga[:, 0:cols] = g_lo[...]
    ga[:, total - cols : total] = g_hi[...]
    for n in range(0, cols, 256):
        grad_out[:, n : n + 256] = dot(lhs[...], onehot[:, n : n + 256])
    for g in range(inner):
        at = slice((g + 1) * cols, (g + 2) * cols)
        new = dot(dec[...], grad_out[g * levels : (g + 1) * levels, :].astype(BF16))
        hid[:, at] = new
        ga[:, at] = new.astype(BF16)

    def finish(i, value):
        hid_out[:, (i - 1) * cols : i * cols] = value

    inner_layers(hid, ga, gb, gate_a, gate_b, w.at[3], w.at[2], near_out, finish)


def mid(incr, key, group, hid_edge, g_lo, g_hi, dec, gate_a, gate_b, w):
    levels, slots = incr.shape
    channels, total = gate_a.shape
    cols = CHUNK * LANES
    inner = total // cols - 2
    sd = jax.ShapeDtypeStruct
    outs = (
        sd((inner * levels, cols), F32),
        sd((channels, inner * cols), F32),
        sd((2, channels, cols), F32),
    )
    return pl.pallas_call(
        mid_kernel,
        in_specs=[VMEM] * 10,
        out_specs=(VMEM,) * 3,
        out_shape=outs,
        scratch_shapes=[
            pltpu.VMEM((channels, total), F32),
            pltpu.VMEM((channels, total), BF16),
            pltpu.VMEM((channels, total), BF16),
            pltpu.VMEM((inner * levels, slots), BF16),
            pltpu.VMEM((slots, cols), BF16),
        ],
        compiler_params=params(24),
        name="mid",
    )(incr, key, group, hid_edge, g_lo, g_hi, dec, gate_a, gate_b, w)


def emit(enc, grad, value, tile):
    full = grad + dot(enc, value.astype(BF16))
    for r in range(CHUNK):
        for l in range(0, full.shape[0], 8):
            tile[pl.ds(l * CHUNK + r, 8, stride=CHUNK), :] = full[
                l : l + 8, r * LANES : (r + 1) * LANES
            ]


def send_tile(tile, out, chunk, sem):
    levels = out.shape[0]
    src = tile.reshape(tile.shape[0] // CHUNK, CHUNK, LANES)
    return pltpu.make_async_copy(
        src.at[0:levels], out.at[:, CHUNK * chunk : CHUNK * (chunk + 1), :], sem
    )


def last_kernel(
    hid_in, hid_edge, g_lo, g_hi, grad, enc, gate_a, gate_b, w,
    out, near_out, hid, ga, gb, tiles, sems,
):
    cols = CHUNK * LANES
    total = hid.shape[1]
    levels = enc.shape[0]
    hid[:, 0:cols] = hid_edge[0]
    hid[:, total - cols : total] = hid_edge[1]
    hid[:, cols : total - cols] = hid_in[...]
    ga[:, 0:cols] = g_lo[...]
    ga[:, total - cols : total] = g_hi[...]
    ga[:, cols : total - cols] = hid_in[...].astype(BF16)
    copies = []

    def finish(i, value):
        slot = (i - 1) % 2
        if i > 2:
            copies[i - 3].wait()
        emit(enc[...], grad[(i - 1) * levels : i * levels, :], value, tiles.at[slot])
        copy = send_tile(tiles.at[slot], out, i, sems.at[slot])
        copy.start()
        copies.append(copy)

    inner_layers(hid, ga, gb, gate_a, gate_b, w.at[1], w.at[0], near_out, finish)
    copies[-2].wait()
    copies[-1].wait()


def last(hid_in, hid_edge, g_lo, g_hi, grad, enc, gate_a, gate_b, w, out_shape):
    channels, total = gate_a.shape
    cols = CHUNK * LANES
    levels = enc.shape[0]
    sd = jax.ShapeDtypeStruct
    return pl.pallas_call(
        last_kernel,
        in_specs=[VMEM] * 9,
        out_specs=(HBM, VMEM),
        out_shape=(sd(out_shape, F32), sd((2, channels, cols), F32)),
        scratch_shapes=[
            pltpu.VMEM((channels, total), F32),
            pltpu.VMEM((channels, total), BF16),
            pltpu.VMEM((channels, total), BF16),
            pltpu.VMEM((2, levels * CHUNK, LANES), F32),
            pltpu.SemaphoreType.DMA((2,)),
        ],
        compiler_params=params(18),
        name="last",
    )(hid_in, hid_edge, g_lo, g_hi, grad, enc, gate_a, gate_b, w)


def edge_values(which, hid, g_lo, g_hi, halo_lo, halo_hi, near, gate_a, gate_b, ah_lo, ah_hi, w):
    cols = CHUNK * LANES
    step = DIL * LANES
    wa, wb = w.at[2 * which + 1], w.at[2 * which]
    total = gate_a.shape[1]
    result = []
    for side in range(2):
        if side == 0:
            field = jnp.concatenate([halo_lo[...], g_lo[...]], axis=1)
            old = jnp.concatenate([halo_lo[:, step:].astype(F32), hid[0, :, :step]], axis=1)
            gate = jnp.concatenate([ah_lo[which], gate_a[:, :step]], axis=1)
        else:
            field = jnp.concatenate([g_hi[...], halo_hi[...]], axis=1)
            old = jnp.concatenate([hid[1, :, step:], halo_hi[:, :step].astype(F32)], axis=1)
            gate = jnp.concatenate([gate_a[:, total - step :], ah_hi[which]], axis=1)
        back = conv(wa, [field[:, d : d + cols] for d in (2 * step, step, 0)])
        new = old + gate.astype(F32) * back
        own = slice(side * (total - cols), side * (total - cols) + cols)
        pieces = (new, near[0]) if side == 0 else (near[1], new)
        joined = jnp.concatenate(pieces, axis=1)
        field = joined.astype(BF16)
        back = conv(wb, [field[:, d : d + cols] for d in (2 * step, step, 0)])
        result.append(joined[:, step : step + cols] + gate_b[:, own].astype(F32) * back)
    return result


def edge_kernel(which, *refs):
    ins, (hid_out, lo_out, hi_out) = refs[:11], refs[12:]
    lo, hi = edge_values(which, *ins)
    hid_out[0] = lo
    hid_out[1] = hi
    lo_out[...] = lo.astype(BF16)
    hi_out[...] = hi.astype(BF16)


def edge_last_kernel(which, *refs):
    ins, (grad, enc, _), (out, tiles, sems) = refs[:11], refs[11:14], refs[14:]
    levels = enc.shape[0]
    values = edge_values(which, *ins)
    chunks = out.shape[1] // CHUNK
    copies = []
    for side in range(2):
        part = grad[side * levels : (side + 1) * levels, :]
        emit(enc[...], part, values[side], tiles.at[side])
        copy = send_tile(tiles.at[side], out, side * (chunks - 1), sems.at[side])
        copy.start()
        copies.append(copy)
    for copy in copies:
        copy.wait()


def edge(which, *args):
    sd = jax.ShapeDtypeStruct
    hid, g_lo = args[:2]
    return pl.pallas_call(
        functools.partial(edge_kernel, which),
        in_specs=[VMEM] * 11 + [ANY],
        out_specs=(VMEM,) * 3,
        out_shape=(sd(hid.shape, F32), sd(g_lo.shape, BF16), sd(g_lo.shape, BF16)),
        compiler_params=params(18),
        name="edge",
    )(*args)


def edge_last(which, *args):
    enc, state = args[12:]
    return pl.pallas_call(
        functools.partial(edge_last_kernel, which),
        in_specs=[VMEM] * 13 + [HBM],
        out_specs=HBM,
        out_shape=jax.ShapeDtypeStruct(state.shape, F32),
        scratch_shapes=[
            pltpu.VMEM((2, enc.shape[0] * CHUNK, LANES), F32),
            pltpu.SemaphoreType.DMA((2,)),
        ],
        input_output_aliases={13: 0},
        compiler_params=params(18),
        name="edge_last",
    )(*args)


def halos(lo, hi):
    count = lax.axis_size("lon")
    up = [(i, (i + 1) % count) for i in range(count)]
    down = [(b, a) for a, b in up]
    return lax.ppermute(hi, "lon", up), lax.ppermute(lo, "lon", down)


def per_device(resid, index, count, weight, jacobian, decoder, conv_weight, gates, encoder):
    dests = lax.axis_size("lat") * lax.axis_size("lon")
    packed = pack(resid, index, count, weight.reshape(1, -1), dests)
    packed = lax.all_to_all(packed, ("lat", "lon"), split_axis=0, concat_axis=0, tiled=True)
    gh_lo, gh_hi = halos(*gate_edges(gates))
    f3, f2, jac, dec, enc, w = prepare(gates, jacobian, decoder, encoder, conv_weight)
    incr, key, group, grad_e, hid_e, g_lo, g_hi = front(packed, jac, dec)
    halo_lo, halo_hi = halos(g_lo, g_hi)
    f1, f0 = later_gates(gates, group)
    grad_i, hid_i, near = mid(incr, key, group, hid_e, g_lo, g_hi, dec, f3, f2, w)
    hid_e, g_lo, g_hi = edge(
        1, hid_e, g_lo, g_hi, halo_lo, halo_hi, near, f3, f2, gh_lo, gh_hi, w, f1
    )
    halo_lo, halo_hi = halos(g_lo, g_hi)
    out_shape = (jacobian.shape[2],) + gates.shape[2:]
    state, near = last(hid_i, hid_e, g_lo, g_hi, grad_i, enc, f1, f0, w, out_shape)
    return edge_last(
        0, hid_e, g_lo, g_hi, halo_lo, halo_hi, near, f1, f0, gh_lo, gh_hi, w, grad_e, enc, state
    )


def solution(mesh):
    return jax.shard_map(
        per_device,
        mesh=mesh,
        in_specs=(
            P(None, ("lat", "lon")),
            P(None, ("lat", "lon")),
            P(None, ("lat", "lon")),
            P(),
            P(),
            P(),
            P(),
            P(None, None, "lon", "lat"),
            P(),
        ),
        out_specs=P(None, "lon", "lat"),
        check_vma=False,
    )
```

```python
import functools

import jax
import jax.numpy as jnp
from jax import lax
from jax.experimental import pallas as pl
from jax.experimental.pallas import tpu as pltpu
from jax.sharding import PartitionSpec as P

F32 = jnp.float32
BF16 = jnp.bfloat16
LANES = 128
CHUNK = 8
DIL = 4
UNUSED = 255.0


def params(mib):
    return pltpu.CompilerParams(vmem_limit_bytes=mib << 20)


def iota(shape, dim):
    return lax.broadcasted_iota(jnp.int32, shape, dim)


def dot(a, b):
    return jnp.dot(a, b, preferred_element_type=F32)


def pack_kernel(resid_hbm, index_hbm, count_hbm, weight_hbm, out_hbm, resid, index, count, weight, out, in_sems, out_sems):
    parts, dests = out.shape[:2]
    slots = resid.shape[2]
    per = slots // dests
    small = [
        pltpu.make_async_copy(index_hbm, index, in_sems.at[parts]),
        pltpu.make_async_copy(count_hbm, count, in_sems.at[parts + 1]),
        pltpu.make_async_copy(weight_hbm, weight, in_sems.at[parts + 2]),
    ]
    for copy in small:
        copy.start()
    large = []
    for p in range(parts):
        src = resid_hbm.at[:, p * slots : (p + 1) * slots]
        large.append(pltpu.make_async_copy(src, resid.at[p], in_sems.at[p]))
        large[-1].start()
    for copy in small:
        copy.wait()
    scale = jnp.broadcast_to(weight[...], (LANES, LANES)).T
    scale = jnp.concatenate([scale] * (slots // LANES), axis=1)
    total = dests * parts
    counts = jnp.broadcast_to(count[...].astype(F32), (8, total)).astype(BF16)
    row = iota((LANES, slots), 0) & 63
    lane = iota((dests, 8, LANES), 2)
    sends = []
    for p in range(parts):
        at = slice(p * slots, (p + 1) * slots)
        spread = iota((total, slots), 1) // per + p * dests == iota((total, slots), 0)
        used = dot(counts, spread.astype(F32).astype(BF16))[0:1]
        cell = index[0:1, at]
        kind = index[1:2, at].astype(F32)
        valid = (iota((1, slots), 1) % per).astype(F32) < used
        low = ((cell >> 7) & (CHUNK - 1)).astype(F32)
        lat = (cell & (LANES - 1)).astype(F32)
        group = jnp.where(valid, (cell >> 10).astype(F32), UNUSED)
        meta = jnp.where(row == 0, low, jnp.where(row == 1, lat, jnp.where(row == 2, group, kind)))
        meta = meta.astype(BF16).T.reshape(dests, 2, 8, LANES)
        first = meta[:, 0].astype(F32)
        second = meta[:, 1].astype(F32)
        out[p, :, per : per + 8, :] = jnp.where(lane < 64, first, second).astype(BF16)
        large[p].wait()
        weighted = scale * resid[p].astype(F32)
        out[p, :, 0:per, :] = weighted.astype(BF16).T.reshape(dests, per, LANES)
        dst = out_hbm.at[p * dests : (p + 1) * dests]
        sends.append(pltpu.make_async_copy(out.at[p], dst, out_sems.at[p]))
        sends[-1].start()
    for copy in sends:
        copy.wait()


HBM = pl.BlockSpec(memory_space=pltpu.HBM)
VMEM = pl.BlockSpec(memory_space=pltpu.VMEM)
ANY = pl.BlockSpec(memory_space=pl.ANY)


def pack(resid, index, count, weight, dests):
    channels, slots = resid.shape
    per = slots // dests
    parts = 4
    return pl.pallas_call(
        pack_kernel,
        in_specs=[HBM] * 4,
        out_specs=HBM,
        out_shape=jax.ShapeDtypeStruct((dests, per + 8, LANES), BF16),
        scratch_shapes=[
            pltpu.VMEM((parts, channels, slots // parts), BF16),
            pltpu.VMEM(index.shape, jnp.int32),
            pltpu.VMEM(count.shape, jnp.int32),
            pltpu.VMEM(weight.shape, F32),
            pltpu.VMEM((parts, dests // parts, per + 8, LANES), BF16),
            pltpu.SemaphoreType.DMA((parts + 3,)),
            pltpu.SemaphoreType.DMA((parts,)),
        ],
        compiler_params=params(63),
        name="pack",
    )(resid, index, count, weight)


def by_channel(wide, lon, pitch, c):
    a = wide[pl.ds(c * pitch + lon, 8, stride=pitch), :]
    b = wide[pl.ds((c + 8) * pitch + lon, 8, stride=pitch), :]
    return jnp.concatenate([a, b], axis=0).astype(BF16)


def prepare_kernel(jac, dec, enc, conv_w, jac_out, dec_out, enc_out, w_out, rows, tall):
    levels, kinds = jac.shape[:2]
    padded = enc_out.shape[0]
    rows[...] = jnp.zeros_like(rows)
    rows[0 : levels * kinds, :] = jac[...].astype(F32).reshape(levels * kinds, LANES)
    for k in range(kinds):
        for l in range(0, padded, 16):
            jac_out[l : l + 16, k * LANES : (k + 1) * LANES] = by_channel(rows, k, kinds, l)
    tall[...] = jnp.zeros_like(tall)
    tall[0:levels, :] = enc[...].astype(F32)
    enc_out[...] = tall[0:padded, :].astype(BF16)
    tall[0:levels, :] = dec[...].astype(F32)
    dec_out[...] = tall[...].T[:, 0:padded].astype(BF16)
    for layer in range(conv_w.shape[0]):
        w_out[layer] = conv_w[layer].T


def prepare(jacobian, decoder, encoder, conv_weight):
    channels, kinds, levels = jacobian.shape
    layers = conv_weight.shape[0]
    padded = levels + -levels % 16
    conv_w = conv_weight.reshape(layers, -1, channels)
    sd = jax.ShapeDtypeStruct
    return pl.pallas_call(
        prepare_kernel,
        in_specs=[VMEM] * 4,
        out_specs=(VMEM,) * 4,
        out_shape=(
            sd((padded, kinds * channels), BF16),
            sd((channels, padded), BF16),
            sd((padded, channels), BF16),
            sd((layers, channels, conv_w.shape[1]), BF16),
        ),
        scratch_shapes=[
            pltpu.VMEM((padded * kinds, channels), F32),
            pltpu.VMEM((256, channels), F32),
        ],
        compiler_params=params(12),
        name="prepare",
    )(jacobian.transpose(2, 1, 0), decoder, encoder.T, conv_w)


def gate_edges_kernel(src, after, lo, hi, buf, wide, sems):
    del after
    channels, lons, lats = src.shape[1:]
    copies = []
    for k in range(2):
        for side in range(2):
            at = side * (lons - CHUNK)
            part = src.at[2 * k + 1, :, at : at + CHUNK, :]
            copies.append(pltpu.make_async_copy(part, buf.at[k, side], sems.at[k, side]))
            copies[-1].start()
    for k in range(2):
        for side, out in enumerate((lo, hi)):
            copies[2 * k + side].wait()
            wide[k, side] = buf[k, side].astype(F32).reshape(channels * CHUNK, lats)
            for r in range(DIL):
                for c in range(0, channels, 16):
                    value = by_channel(wide.at[k, side], side * DIL + r, CHUNK, c)
                    out[k, c : c + 16, r * lats : (r + 1) * lats] = value


def gate_edges(gates, after):
    layers, channels, lons, lats = gates.shape
    send = jax.ShapeDtypeStruct((2, channels, DIL * lats), BF16)
    return pl.pallas_call(
        gate_edges_kernel,
        in_specs=[HBM, ANY],
        out_specs=(VMEM,) * 2,
        out_shape=(send,) * 2,
        scratch_shapes=[
            pltpu.VMEM((2, 2, channels, CHUNK, lats), BF16),
            pltpu.VMEM((2, 2, channels * CHUNK, lats), F32),
            pltpu.SemaphoreType.DMA((2, 2)),
        ],
        compiler_params=params(58),
        name="gate_edges",
    )(gates, after)


def front_kernel(packed, jac, dec, incr_out, key_out, group_out, grad_out, hid_out, lo_out, hi_out):
    senders = packed.shape[0]
    half = senders * 8
    slots = 2 * half
    levels = jac.shape[0]
    kinds = jac.shape[1] // LANES
    x = jnp.concatenate(
        [packed[:, 0:8, :].reshape(half, LANES).T, packed[:, 8:16, :].reshape(half, LANES).T],
        axis=1,
    )
    meta = packed[:, 16:24, :].reshape(half, LANES)
    meta_t = meta.astype(F32).T

    def line(q):
        return jnp.concatenate([meta_t[q : q + 1], meta_t[64 + q : 65 + q]], axis=1)

    def column(q):
        pick = iota((LANES, LANES), 0)
        a = dot(meta, (pick == q).astype(F32).astype(BF16))
        b = dot(meta, (pick == 64 + q).astype(F32).astype(BF16))
        return jnp.concatenate([a, b], axis=0)

    group = line(2)
    kind = line(3)
    group_out[...] = jnp.broadcast_to(group, (8, slots))
    spread = jnp.concatenate(
        [x * (kind == k).astype(F32).astype(BF16) for k in range(kinds)], axis=0
    )
    incr = dot(jac[...], spread).astype(BF16)
    incr_out[...] = incr
    key = column(0) * LANES + column(1) - iota((slots, LANES), 1).astype(F32)
    key_out[...] = key
    onehot = hot(key)
    last = CHUNK - 1
    lhs = jnp.concatenate(
        [incr * (group == g).astype(F32).astype(BF16) for g in (0, last)], axis=0
    )
    grad = dot(lhs, onehot)
    grad_out[...] = grad
    for side in range(2):
        part = grad[side * levels : (side + 1) * levels].astype(BF16)
        hidden = dot(dec[...], part)
        hid_out[side] = hidden
        (lo_out, hi_out)[side][...] = hidden.astype(BF16)


def hot(key):
    return jnp.concatenate(
        [jnp.where(key == float(r * LANES), 1.0, 0.0).astype(BF16) for r in range(CHUNK)], axis=1
    )


def front(packed, jac, dec):
    slots = packed.shape[0] * 16
    levels = jac.shape[0]
    cols = CHUNK * LANES
    sd = jax.ShapeDtypeStruct
    return pl.pallas_call(
        front_kernel,
        in_specs=[VMEM] * 3,
        out_specs=(VMEM,) * 7,
        out_shape=(
            sd((levels, slots), BF16),
            sd((slots, LANES), F32),
            sd((8, slots), F32),
            sd((2 * levels, cols), F32),
            sd((2, LANES, cols), F32),
            sd((LANES, cols), BF16),
            sd((LANES, cols), BF16),
        ),
        compiler_params=params(28),
        name="front",
    )(packed, jac, dec)


def conv(weight, taps):
    return dot(weight[...], jnp.concatenate(taps, axis=0))


def pieces(low, inside, high, start, size):
    parts = []
    at = 0
    for ref in (low, inside, high):
        first, stop = max(start - at, 0), min(start + size - at, ref.shape[1])
        if first < stop:
            parts.append(ref[:, first:stop])
        at += ref.shape[1]
    return parts[0] if len(parts) == 1 else jnp.concatenate(parts, axis=1)


def load_gates(gates, layer, bufs, sems):
    copies = [
        pltpu.make_async_copy(gates.at[layer - i], bufs.at[i], sems.at[i]) for i in range(2)
    ]
    for copy in copies:
        copy.start()
    return copies


def widen(copy, buf, wide):
    channels, lons = buf.shape[:2]
    pitch = wide.shape[0] // channels
    copy.wait()

    def body(c, carry):
        wide[pl.ds(pl.multiple_of(c * pitch, 8), lons), :] = buf[c].astype(F32)
        return carry

    lax.fori_loop(0, channels, body, 0, unroll=8)


def gate_rows(wide, lon, count, channels):
    pitch = wide.shape[0] // channels
    columns = [
        jnp.concatenate(
            [wide[pl.ds(c * pitch + r, 8, stride=pitch), :] for c in range(0, channels, 8)], axis=0
        )
        for r in range(lon, lon + count)
    ]
    return jnp.concatenate(columns, axis=1)


def inner_layers(low, inside, high, old, hid, gb, load, bufs, wide, wa, wb, near_out, finish, ends=None):
    cols = CHUNK * LANES
    step = DIL * LANES
    channels, total = hid.shape
    count = total // cols
    widen(load[0], bufs.at[0], wide)
    for i in range(count - 1):
        o = step + i * cols
        at = slice(o, o + cols)
        taps = [pieces(low, inside, high, o + d, cols) for d in (step, 0, -step)]
        back = conv(wa, taps)
        new = old(o, cols) + gate_rows(wide, o // LANES, CHUNK, channels) * back
        hid[:, at] = new
        gb[:, at] = new.astype(BF16)
    near_out[0] = hid[:, step : step + cols]
    near_out[1] = hid[:, total - step - cols : total - step]
    lons = total // LANES
    if ends is not None:
        ends[0] = gate_rows(wide, 0, DIL, channels).astype(BF16)
        ends[1] = gate_rows(wide, lons - DIL, DIL, channels).astype(BF16)
    widen(load[1], bufs.at[1], wide)
    for i in range(1, count - 1):
        o = i * cols
        at = slice(o, o + cols)
        back = conv(wb, [gb[:, o + d : o + d + cols] for d in (step, 0, -step)])
        finish(i, hid[:, at] + gate_rows(wide, o // LANES, CHUNK, channels) * back)


def mid_kernel(
    incr, key, group, hid_edge, g_lo, g_hi, dec, gates, w,
    grad_out, hid_out, field_out, near_out, ends_a, ends_b,
    hid, ga, gb, lhs, onehot, bufs, wide, sems,
):
    load = load_gates(gates, 3, bufs, sems)
    cols = CHUNK * LANES
    step = DIL * LANES
    levels = incr.shape[0]
    channels, total = hid.shape
    inner = total // cols - 2
    onehot[...] = hot(key[...])
    for g in range(inner):
        mask = (group[0:1, :] == float(g + 1)).astype(F32).astype(BF16)
        lhs[g * levels : (g + 1) * levels, :] = incr[...] * mask
    hid[:, 0:cols] = hid_edge[0]
    hid[:, total - cols : total] = hid_edge[1]
    for n in range(0, cols, 256):
        grad_out[:, n : n + 256] = dot(lhs[...], onehot[:, n : n + 256])
    for g in range(inner):
        new = dot(dec[...], grad_out[g * levels : (g + 1) * levels, :].astype(BF16))
        hid[:, (g + 1) * cols : (g + 2) * cols] = new
        ga[:, g * cols : (g + 1) * cols] = new.astype(BF16)

    def old(o, size):
        return hid[:, o : o + size]

    def finish(i, value):
        hid_out[:, (i - 1) * cols : i * cols] = value
        field_out[:, (i - 1) * cols : i * cols] = value.astype(BF16)

    inner_layers(
        g_lo, ga, g_hi, old, hid, gb, load, bufs, wide, w.at[3], w.at[2], near_out, finish, ends_a
    )
    lons = total // LANES
    ends_b[0] = gate_rows(wide, 0, CHUNK, channels).astype(BF16)
    ends_b[1] = gate_rows(wide, lons - CHUNK, CHUNK, channels).astype(BF16)


def gates_scratch(gates):
    channels, lons, lats = gates.shape[1:]
    return [
        pltpu.VMEM((2, channels, lons, lats), BF16),
        pltpu.VMEM((channels * (lons + 8), lats), F32),
        pltpu.SemaphoreType.DMA((2,)),
    ]


def mid(incr, key, group, hid_edge, g_lo, g_hi, dec, gates, w):
    levels, slots = incr.shape
    channels, lons, lats = gates.shape[1:]
    total = lons * lats
    cols = CHUNK * LANES
    inner = total // cols - 2
    sd = jax.ShapeDtypeStruct
    outs = (
        sd((inner * levels, cols), F32),
        sd((channels, inner * cols), F32),
        sd((channels, inner * cols), BF16),
        sd((2, channels, cols), F32),
        sd((2, channels, DIL * LANES), BF16),
        sd((2, channels, cols), BF16),
    )
    return pl.pallas_call(
        mid_kernel,
        in_specs=[VMEM] * 7 + [HBM, VMEM],
        out_specs=(VMEM,) * 6,
        out_shape=outs,
        scratch_shapes=[
            pltpu.VMEM((channels, total), F32),
            pltpu.VMEM((channels, inner * cols), BF16),
            pltpu.VMEM((channels, total), BF16),
            pltpu.VMEM((inner * levels, slots), BF16),
            pltpu.VMEM((slots, cols), BF16),
        ]
        + gates_scratch(gates),
        compiler_params=params(44),
        name="mid",
    )(incr, key, group, hid_edge, g_lo, g_hi, dec, gates, w)


def emit(enc, grad, value, tile):
    full = grad + dot(enc, value.astype(BF16))
    for r in range(CHUNK):
        for l in range(0, full.shape[0], 8):
            tile[pl.ds(l * CHUNK + r, 8, stride=CHUNK), :] = full[
                l : l + 8, r * LANES : (r + 1) * LANES
            ]


def send_tile(tile, out, chunk, sem):
    levels = out.shape[0]
    src = tile.reshape(tile.shape[0] // CHUNK, CHUNK, LANES)
    return pltpu.make_async_copy(
        src.at[0:levels], out.at[:, CHUNK * chunk : CHUNK * (chunk + 1), :], sem
    )


def last_kernel(
    hid_in, field_in, hid_edge, g_lo, g_hi, grad, enc, gates, w,
    out, near_out, ends_a, ends_b, hid, gb, tiles, sems, bufs, wide, gate_sems,
):
    load = load_gates(gates, 1, bufs, gate_sems)
    cols = CHUNK * LANES
    channels, total = hid.shape
    levels = enc.shape[0]
    copies = []

    def old(o, size):
        return pieces(hid_edge.at[0], hid_in, hid_edge.at[1], o, size)

    def finish(i, value):
        slot = (i - 1) % 2
        if i > 2:
            copies[i - 3].wait()
        emit(enc[...], grad[(i - 1) * levels : i * levels, :], value, tiles.at[slot])
        copy = send_tile(tiles.at[slot], out, i, sems.at[slot])
        copy.start()
        copies.append(copy)

    inner_layers(
        g_lo, field_in, g_hi, old, hid, gb, load, bufs, wide, w.at[1], w.at[0], near_out, finish, ends_a
    )
    lons = total // LANES
    ends_b[0] = gate_rows(wide, 0, CHUNK, channels).astype(BF16)
    ends_b[1] = gate_rows(wide, lons - CHUNK, CHUNK, channels).astype(BF16)
    copies[-2].wait()
    copies[-1].wait()


def last(hid_in, field_in, hid_edge, g_lo, g_hi, grad, enc, gates, w, out_shape):
    channels, lons, lats = gates.shape[1:]
    total = lons * lats
    cols = CHUNK * LANES
    levels = enc.shape[0]
    sd = jax.ShapeDtypeStruct
    return pl.pallas_call(
        last_kernel,
        in_specs=[VMEM] * 7 + [HBM, VMEM],
        out_specs=(HBM, VMEM, VMEM, VMEM),
        out_shape=(
            sd(out_shape, F32),
            sd((2, channels, cols), F32),
            sd((2, channels, DIL * LANES), BF16),
            sd((2, channels, cols), BF16),
        ),
        scratch_shapes=[
            pltpu.VMEM((channels, total), F32),
            pltpu.VMEM((channels, total), BF16),
            pltpu.VMEM((2, levels * CHUNK, LANES), F32),
            pltpu.SemaphoreType.DMA((2,)),
        ]
        + gates_scratch(gates),
        compiler_params=params(46),
        name="last",
    )(hid_in, field_in, hid_edge, g_lo, g_hi, grad, enc, gates, w)


def edge_values(which, hid, g_lo, g_hi, halo_lo, halo_hi, near, gate_a, gate_b, ah_lo, ah_hi, w):
    cols = CHUNK * LANES
    step = DIL * LANES
    wa, wb = w.at[2 * which + 1], w.at[2 * which]
    result = []
    for side in range(2):
        if side == 0:
            field = jnp.concatenate([halo_lo[...], g_lo[...]], axis=1)
            old = jnp.concatenate([halo_lo[:, step:].astype(F32), hid[0, :, :step]], axis=1)
            gate = jnp.concatenate([ah_lo[which], gate_a[0]], axis=1)
        else:
            field = jnp.concatenate([g_hi[...], halo_hi[...]], axis=1)
            old = jnp.concatenate([hid[1, :, step:], halo_hi[:, :step].astype(F32)], axis=1)
            gate = jnp.concatenate([gate_a[1], ah_hi[which]], axis=1)
        back = conv(wa, [field[:, d : d + cols] for d in (2 * step, step, 0)])
        new = old + gate.astype(F32) * back
        pieces = (new, near[0]) if side == 0 else (near[1], new)
        joined = jnp.concatenate(pieces, axis=1)
        field = joined.astype(BF16)
        back = conv(wb, [field[:, d : d + cols] for d in (2 * step, step, 0)])
        result.append(joined[:, step : step + cols] + gate_b[side].astype(F32) * back)
    return result


def edge_kernel(which, *refs):
    ins, (hid_out, lo_out, hi_out) = refs[:11], refs[11:]
    lo, hi = edge_values(which, *ins)
    hid_out[0] = lo
    hid_out[1] = hi
    lo_out[...] = lo.astype(BF16)
    hi_out[...] = hi.astype(BF16)


def edge_last_kernel(which, *refs):
    ins, (grad, enc, _), (out, tiles, sems) = refs[:11], refs[11:14], refs[14:]
    levels = enc.shape[0]
    values = edge_values(which, *ins)
    chunks = out.shape[1] // CHUNK
    copies = []
    for side in range(2):
        part = grad[side * levels : (side + 1) * levels, :]
        emit(enc[...], part, values[side], tiles.at[side])
        copy = send_tile(tiles.at[side], out, side * (chunks - 1), sems.at[side])
        copy.start()
        copies.append(copy)
    for copy in copies:
        copy.wait()


def edge(which, *args):
    sd = jax.ShapeDtypeStruct
    hid, g_lo = args[:2]
    return pl.pallas_call(
        functools.partial(edge_kernel, which),
        in_specs=[VMEM] * 11,
        out_specs=(VMEM,) * 3,
        out_shape=(sd(hid.shape, F32), sd(g_lo.shape, BF16), sd(g_lo.shape, BF16)),
        compiler_params=params(18),
        name="edge",
    )(*args)


def edge_last(which, *args):
    enc, state = args[12:]
    return pl.pallas_call(
        functools.partial(edge_last_kernel, which),
        in_specs=[VMEM] * 13 + [HBM],
        out_specs=HBM,
        out_shape=jax.ShapeDtypeStruct(state.shape, F32),
        scratch_shapes=[
            pltpu.VMEM((2, enc.shape[0] * CHUNK, LANES), F32),
            pltpu.SemaphoreType.DMA((2,)),
        ],
        input_output_aliases={13: 0},
        compiler_params=params(18),
        name="edge_last",
    )(*args)


def halos(lo, hi):
    count = lax.axis_size("lon")
    up = [(i, (i + 1) % count) for i in range(count)]
    down = [(b, a) for a, b in up]
    return lax.ppermute(hi, "lon", up), lax.ppermute(lo, "lon", down)


def per_device(resid, index, count, weight, jacobian, decoder, conv_weight, gates, encoder):
    dests = lax.axis_size("lat") * lax.axis_size("lon")
    packed = pack(resid, index, count, weight.reshape(1, -1), dests)
    packed = lax.all_to_all(packed, ("lat", "lon"), split_axis=0, concat_axis=0, tiled=True)
    jac, dec, enc, w = prepare(jacobian, decoder, encoder, conv_weight)
    gh_lo, gh_hi = halos(*gate_edges(gates, dec))
    incr, key, group, grad_e, hid_e, g_lo, g_hi = front(packed, jac, dec)
    halo_lo, halo_hi = halos(g_lo, g_hi)
    grad_i, hid_i, field_i, near, end_a, end_b = mid(
        incr, key, group, hid_e, g_lo, g_hi, dec, gates, w
    )
    hid_e, g_lo, g_hi = edge(
        1, hid_e, g_lo, g_hi, halo_lo, halo_hi, near, end_a, end_b, gh_lo, gh_hi, w
    )
    halo_lo, halo_hi = halos(g_lo, g_hi)
    out_shape = (jacobian.shape[2],) + gates.shape[2:]
    state, near, end_a, end_b = last(
        hid_i, field_i, hid_e, g_lo, g_hi, grad_i, enc, gates, w, out_shape
    )
    return edge_last(
        0, hid_e, g_lo, g_hi, halo_lo, halo_hi, near, end_a, end_b, gh_lo, gh_hi, w,
        grad_e, enc, state,
    )


def solution(mesh):
    return jax.shard_map(
        per_device,
        mesh=mesh,
        in_specs=(
            P(None, ("lat", "lon")),
            P(None, ("lat", "lon")),
            P(None, ("lat", "lon")),
            P(),
            P(),
            P(),
            P(),
            P(None, None, "lon", "lat"),
            P(),
        ),
        out_specs=P(None, "lon", "lat"),
        check_vma=False,
    )
```

```python
import functools

import jax
import jax.numpy as jnp
from jax import lax
from jax.experimental import pallas as pl
from jax.experimental.pallas import tpu as pltpu
from jax.sharding import PartitionSpec as P

F32 = jnp.float32
BF16 = jnp.bfloat16
LANES = 128
CHUNK = 8
DIL = 4
UNUSED = 255.0


def params(mib):
    return pltpu.CompilerParams(vmem_limit_bytes=mib << 20)


def iota(shape, dim):
    return lax.broadcasted_iota(jnp.int32, shape, dim)


def dot(a, b):
    return jnp.dot(a, b, preferred_element_type=F32)


def pack_kernel(resid_hbm, index_hbm, count_hbm, weight_hbm, out_hbm, resid, index, count, weight, out, in_sems, out_sems):
    parts, dests = out.shape[:2]
    slots = resid.shape[2]
    per = slots // dests
    pairs = per // 2
    small = [
        pltpu.make_async_copy(index_hbm, index, in_sems.at[parts]),
        pltpu.make_async_copy(count_hbm, count, in_sems.at[parts + 1]),
        pltpu.make_async_copy(weight_hbm, weight, in_sems.at[parts + 2]),
    ]
    for copy in small:
        copy.start()
    large = []
    for p in range(parts):
        src = resid_hbm.at[:, p * slots : (p + 1) * slots]
        large.append(pltpu.make_async_copy(src, resid.at[p], in_sems.at[p]))
        large[-1].start()
    width = LANES // pairs
    row = iota((LANES, slots), 0) & (width - 1)
    lane, slot = iota((LANES, slots), 0), iota((LANES, slots), 1)
    mine = ((slot & (per - 1)) >> 1) == (lane >> (width.bit_length() - 1))
    shift = per.bit_length() - 1
    fold_to, fold_from = iota((2 * dests, slots), 0), iota((2 * dests, slots), 1)
    fold = ((fold_from >> shift) * 2 + (fold_from & 1)) == fold_to
    fold = fold.astype(F32).astype(BF16)
    own = (iota((dests, slots), 1) >> shift) == iota((dests, slots), 0)
    own = own.astype(F32).astype(BF16)
    place = (iota((1, slots), 1) & (per - 1)).astype(F32)
    total = dests * parts
    for copy in small:
        copy.wait()
    scale = jnp.broadcast_to(weight[...], (LANES, LANES)).T
    scale = jnp.concatenate([scale] * (slots // LANES), axis=1)
    counts = jnp.broadcast_to(count[...].astype(F32), (8, total)).astype(BF16)
    for copy in large:
        copy.wait()
    sends = []
    for p in range(parts):
        at = slice(p * slots, (p + 1) * slots)
        used = dot(counts[:, p * dests : (p + 1) * dests], own)[0:1]
        cell = index[0:1, at]
        kind = index[1:2, at].astype(F32)
        valid = place < used
        low = ((cell >> 7) & (CHUNK - 1)).astype(F32)
        lat = (cell & (LANES - 1)).astype(F32)
        group = jnp.where(valid, (cell >> 10).astype(F32), UNUSED)
        meta = jnp.where(row == 0, low, jnp.where(row == 1, lat, jnp.where(row == 2, group, kind)))
        meta = jnp.where(mine, meta, 0.0).astype(BF16)
        meta = lax.dot_general(fold, meta, (((1,), (1,)), ((), ())), preferred_element_type=F32)
        out[p, :, pairs : pairs + 1] = meta.astype(BF16).reshape(dests, 1, 2, LANES)
        weighted = scale * resid[p].astype(F32)
        out[p, :, 0:pairs] = weighted.astype(BF16).T.reshape(dests, pairs, 2, LANES)
    for p in range(parts):
        dst = out_hbm.at[p * dests : (p + 1) * dests]
        sends.append(pltpu.make_async_copy(out.at[p], dst, out_sems.at[p]))
        sends[-1].start()
    for copy in sends:
        copy.wait()


HBM = pl.BlockSpec(memory_space=pltpu.HBM)
VMEM = pl.BlockSpec(memory_space=pltpu.VMEM)
ANY = pl.BlockSpec(memory_space=pl.ANY)


def pack(resid, index, count, weight, dests):
    channels, slots = resid.shape
    per = slots // dests
    parts = 4
    return pl.pallas_call(
        pack_kernel,
        in_specs=[HBM] * 4,
        out_specs=HBM,
        out_shape=jax.ShapeDtypeStruct((dests, per // 2 + 1, 2, LANES), BF16),
        scratch_shapes=[
            pltpu.VMEM((parts, channels, slots // parts), BF16),
            pltpu.VMEM(index.shape, jnp.int32),
            pltpu.VMEM(count.shape, jnp.int32),
            pltpu.VMEM(weight.shape, F32),
            pltpu.VMEM((parts, dests // parts, per // 2 + 1, 2, LANES), BF16),
            pltpu.SemaphoreType.DMA((parts + 3,)),
            pltpu.SemaphoreType.DMA((parts,)),
        ],
        compiler_params=params(63),
        name="pack",
    )(resid, index, count, weight)


def by_channel(wide, lon, pitch, c):
    a = wide[pl.ds(c * pitch + lon, 8, stride=pitch), :]
    b = wide[pl.ds((c + 8) * pitch + lon, 8, stride=pitch), :]
    return jnp.concatenate([a, b], axis=0).astype(BF16)


def prepare_kernel(jac, dec, enc, conv_w, after, jac_out, dec_out, enc_out, w_out, rows, tall):
    del after
    levels, kinds = jac.shape[:2]
    padded = enc_out.shape[0]
    rows[...] = jnp.zeros_like(rows)
    rows[0 : levels * kinds, :] = jac[...].astype(F32).reshape(levels * kinds, LANES)
    for k in range(kinds):
        for l in range(0, padded, 16):
            jac_out[l : l + 16, k * LANES : (k + 1) * LANES] = by_channel(rows, k, kinds, l)
    tall[...] = jnp.zeros_like(tall)
    tall[0:levels, :] = enc[...].astype(F32)
    enc_out[...] = tall[0:padded, :].astype(BF16)
    tall[0:levels, :] = dec[...].astype(F32)
    dec_out[...] = tall[...].T[:, 0:padded].astype(BF16)
    for layer in range(conv_w.shape[0]):
        w_out[layer] = conv_w[layer].T


def prepare(jacobian, decoder, encoder, conv_weight, after):
    channels, kinds, levels = jacobian.shape
    layers = conv_weight.shape[0]
    padded = levels + -levels % 16
    conv_w = conv_weight.reshape(layers, -1, channels)
    sd = jax.ShapeDtypeStruct
    return pl.pallas_call(
        prepare_kernel,
        in_specs=[VMEM] * 4 + [ANY],
        out_specs=(VMEM,) * 4,
        out_shape=(
            sd((padded, kinds * channels), BF16),
            sd((channels, padded), BF16),
            sd((padded, channels), BF16),
            sd((layers, channels, conv_w.shape[1]), BF16),
        ),
        scratch_shapes=[
            pltpu.VMEM((padded * kinds, channels), F32),
            pltpu.VMEM((256, channels), F32),
        ],
        compiler_params=params(20),
        name="prepare",
    )(jacobian.transpose(2, 1, 0), decoder, encoder.T, conv_w, after)


def gate_edges_kernel(src, lo, hi, buf, wide, sems):
    channels, lons, lats = src.shape[1:]
    copies = []
    for k in range(2):
        for side in range(2):
            at = side * (lons - CHUNK)
            part = src.at[2 * k + 1, :, at : at + CHUNK, :]
            copies.append(pltpu.make_async_copy(part, buf.at[k, side], sems.at[k, side]))
            copies[-1].start()
    for k in range(2):
        for side, out in enumerate((lo, hi)):
            copies[2 * k + side].wait()
            wide[k, side] = buf[k, side].astype(F32).reshape(channels * CHUNK, lats)
            for r in range(DIL):
                for c in range(0, channels, 16):
                    value = by_channel(wide.at[k, side], side * DIL + r, CHUNK, c)
                    out[k, c : c + 16, r * lats : (r + 1) * lats] = value


def gate_edges(gates):
    layers, channels, lons, lats = gates.shape
    send = jax.ShapeDtypeStruct((2, channels, DIL * lats), BF16)
    return pl.pallas_call(
        gate_edges_kernel,
        in_specs=[HBM],
        out_specs=(VMEM,) * 2,
        out_shape=(send,) * 2,
        scratch_shapes=[
            pltpu.VMEM((2, 2, channels, CHUNK, lats), BF16),
            pltpu.VMEM((2, 2, channels * CHUNK, lats), F32),
            pltpu.SemaphoreType.DMA((2, 2)),
        ],
        compiler_params=params(58),
        name="gate_edges",
    )(gates)


def front_kernel(packed, jac, dec, incr_out, key_out, group_out, grad_out, hid_out, lo_out, hi_out):
    senders, pairs = packed.shape[0], packed.shape[1] - 1
    part = 2 * senders
    slots = pairs * part
    width = LANES // pairs
    levels = jac.shape[0]
    kinds = jac.shape[1] // LANES
    x = jnp.concatenate([packed[:, m].reshape(part, LANES).T for m in range(pairs)], axis=1)
    meta = packed[:, pairs].reshape(part, LANES)
    meta_t = meta.astype(F32).T

    def line(q):
        rows = [m * width + q for m in range(pairs)]
        return jnp.concatenate([meta_t[r : r + 1] for r in rows], axis=1)

    def place(m):
        source = iota((LANES, LANES), 0) - m * width
        pick = jnp.where(source == 0, float(LANES), jnp.where(source == 1, 1.0, 0.0))
        return dot(meta, pick.astype(BF16))

    group = line(2)
    kind = line(3)
    group_out[...] = jnp.broadcast_to(group, (8, slots))
    spread = jnp.concatenate(
        [x * (kind == k).astype(F32).astype(BF16) for k in range(kinds)], axis=0
    )
    incr = dot(jac[...], spread).astype(BF16)
    incr_out[...] = incr
    key = jnp.concatenate([place(m) for m in range(pairs)], axis=0)
    key = key - iota((slots, LANES), 1).astype(F32)
    key_out[...] = key
    onehot = hot(key)
    last = CHUNK - 1
    lhs = jnp.concatenate(
        [incr * (group == g).astype(F32).astype(BF16) for g in (0, last)], axis=0
    )
    grad = dot(lhs, onehot)
    grad_out[...] = grad
    for side in range(2):
        part = grad[side * levels : (side + 1) * levels].astype(BF16)
        hidden = dot(dec[...], part)
        hid_out[side] = hidden
        (lo_out, hi_out)[side][...] = hidden.astype(BF16)


def hot(key):
    return jnp.concatenate(
        [jnp.where(key == float(r * LANES), 1.0, 0.0).astype(BF16) for r in range(CHUNK)], axis=1
    )


def front(packed, jac, dec):
    slots = packed.shape[0] * (packed.shape[1] - 1) * 2
    levels = jac.shape[0]
    cols = CHUNK * LANES
    sd = jax.ShapeDtypeStruct
    return pl.pallas_call(
        front_kernel,
        in_specs=[VMEM] * 3,
        out_specs=(VMEM,) * 7,
        out_shape=(
            sd((levels, slots), BF16),
            sd((slots, LANES), F32),
            sd((8, slots), F32),
            sd((2 * levels, cols), F32),
            sd((2, LANES, cols), F32),
            sd((LANES, cols), BF16),
            sd((LANES, cols), BF16),
        ),
        compiler_params=params(28),
        name="front",
    )(packed, jac, dec)


def conv(weight, taps):
    return dot(weight[...], jnp.concatenate(taps, axis=0))


def pieces(low, inside, high, start, size):
    parts = []
    at = 0
    for ref in (low, inside, high):
        first, stop = max(start - at, 0), min(start + size - at, ref.shape[1])
        if first < stop:
            parts.append(ref[:, first:stop])
        at += ref.shape[1]
    return parts[0] if len(parts) == 1 else jnp.concatenate(parts, axis=1)


def load_gates(gates, layer, bufs, sems):
    copies = [
        pltpu.make_async_copy(gates.at[layer - i], bufs.at[i], sems.at[i]) for i in range(2)
    ]
    for copy in copies:
        copy.start()
    return copies


def widen(copy, buf, wide):
    channels, lons = buf.shape[:2]
    pitch = wide.shape[0] // channels
    copy.wait()

    def body(c, carry):
        wide[pl.ds(pl.multiple_of(c * pitch, 8), lons), :] = buf[c].astype(F32)
        return carry

    lax.fori_loop(0, channels, body, 0, unroll=8)


def gate_rows(wide, lon, count, channels):
    pitch = wide.shape[0] // channels
    columns = [
        jnp.concatenate(
            [wide[pl.ds(c * pitch + r, 8, stride=pitch), :] for c in range(0, channels, 8)], axis=0
        )
        for r in range(lon, lon + count)
    ]
    return jnp.concatenate(columns, axis=1)


def inner_layers(low, inside, high, old, hid, gb, load, bufs, wide, wa, wb, near_out, finish, ends=None):
    cols = CHUNK * LANES
    step = DIL * LANES
    channels, total = hid.shape
    count = total // cols
    widen(load[0], bufs.at[0], wide)
    for i in range(count - 1):
        o = step + i * cols
        at = slice(o, o + cols)
        taps = [pieces(low, inside, high, o + d, cols) for d in (step, 0, -step)]
        back = conv(wa, taps)
        new = old(o, cols) + gate_rows(wide, o // LANES, CHUNK, channels) * back
        hid[:, at] = new
        gb[:, at] = new.astype(BF16)
    near_out[0] = hid[:, step : step + cols]
    near_out[1] = hid[:, total - step - cols : total - step]
    lons = total // LANES
    if ends is not None:
        ends[0] = gate_rows(wide, 0, DIL, channels).astype(BF16)
        ends[1] = gate_rows(wide, lons - DIL, DIL, channels).astype(BF16)
    widen(load[1], bufs.at[1], wide)
    for i in range(1, count - 1):
        o = i * cols
        at = slice(o, o + cols)
        back = conv(wb, [gb[:, o + d : o + d + cols] for d in (step, 0, -step)])
        finish(i, hid[:, at] + gate_rows(wide, o // LANES, CHUNK, channels) * back)


def mid_kernel(
    incr, key, group, hid_edge, g_lo, g_hi, dec, gates, w,
    grad_out, hid_out, field_out, near_out, ends_a, ends_b,
    hid, ga, gb, lhs, onehot, bufs, wide, sems,
):
    load = load_gates(gates, 3, bufs, sems)
    cols = CHUNK * LANES
    step = DIL * LANES
    levels = incr.shape[0]
    channels, total = hid.shape
    inner = total // cols - 2
    onehot[...] = hot(key[...])
    for g in range(inner):
        mask = (group[0:1, :] == float(g + 1)).astype(F32).astype(BF16)
        lhs[g * levels : (g + 1) * levels, :] = incr[...] * mask
    hid[:, 0:cols] = hid_edge[0]
    hid[:, total - cols : total] = hid_edge[1]
    for n in range(0, cols, 256):
        grad_out[:, n : n + 256] = dot(lhs[...], onehot[:, n : n + 256])
    for g in range(inner):
        new = dot(dec[...], grad_out[g * levels : (g + 1) * levels, :].astype(BF16))
        hid[:, (g + 1) * cols : (g + 2) * cols] = new
        ga[:, g * cols : (g + 1) * cols] = new.astype(BF16)

    def old(o, size):
        return hid[:, o : o + size]

    def finish(i, value):
        hid_out[:, (i - 1) * cols : i * cols] = value
        field_out[:, (i - 1) * cols : i * cols] = value.astype(BF16)

    inner_layers(
        g_lo, ga, g_hi, old, hid, gb, load, bufs, wide, w.at[3], w.at[2], near_out, finish, ends_a
    )
    lons = total // LANES
    ends_b[0] = gate_rows(wide, 0, CHUNK, channels).astype(BF16)
    ends_b[1] = gate_rows(wide, lons - CHUNK, CHUNK, channels).astype(BF16)


def gates_scratch(gates):
    channels, lons, lats = gates.shape[1:]
    return [
        pltpu.VMEM((2, channels, lons, lats), BF16),
        pltpu.VMEM((channels * (lons + 8), lats), F32),
        pltpu.SemaphoreType.DMA((2,)),
    ]


def mid(incr, key, group, hid_edge, g_lo, g_hi, dec, gates, w):
    levels, slots = incr.shape
    channels, lons, lats = gates.shape[1:]
    total = lons * lats
    cols = CHUNK * LANES
    inner = total // cols - 2
    sd = jax.ShapeDtypeStruct
    outs = (
        sd((inner * levels, cols), F32),
        sd((channels, inner * cols), F32),
        sd((channels, inner * cols), BF16),
        sd((2, channels, cols), F32),
        sd((2, channels, DIL * LANES), BF16),
        sd((2, channels, cols), BF16),
    )
    return pl.pallas_call(
        mid_kernel,
        in_specs=[VMEM] * 7 + [HBM, VMEM],
        out_specs=(VMEM,) * 6,
        out_shape=outs,
        scratch_shapes=[
            pltpu.VMEM((channels, total), F32),
            pltpu.VMEM((channels, inner * cols), BF16),
            pltpu.VMEM((channels, total), BF16),
            pltpu.VMEM((inner * levels, slots), BF16),
            pltpu.VMEM((slots, cols), BF16),
        ]
        + gates_scratch(gates),
        compiler_params=params(40),
        name="mid",
    )(incr, key, group, hid_edge, g_lo, g_hi, dec, gates, w)


def emit(enc, grad, value, tile):
    full = grad + dot(enc, value.astype(BF16))
    for r in range(CHUNK):
        for l in range(0, full.shape[0], 8):
            tile[pl.ds(l * CHUNK + r, 8, stride=CHUNK), :] = full[
                l : l + 8, r * LANES : (r + 1) * LANES
            ]


def send_tile(tile, out, chunk, sem):
    levels = out.shape[0]
    src = tile.reshape(tile.shape[0] // CHUNK, CHUNK, LANES)
    return pltpu.make_async_copy(
        src.at[0:levels], out.at[:, CHUNK * chunk : CHUNK * (chunk + 1), :], sem
    )


def last_kernel(
    hid_in, field_in, hid_edge, g_lo, g_hi, grad, enc, gates, w,
    out, near_out, ends_a, ends_b, hid, gb, tiles, sems, bufs, wide, gate_sems,
):
    load = load_gates(gates, 1, bufs, gate_sems)
    cols = CHUNK * LANES
    channels, total = hid.shape
    levels = enc.shape[0]
    copies = []

    def old(o, size):
        return pieces(hid_edge.at[0], hid_in, hid_edge.at[1], o, size)

    def finish(i, value):
        slot = (i - 1) % 2
        if i > 2:
            copies[i - 3].wait()
        emit(enc[...], grad[(i - 1) * levels : i * levels, :], value, tiles.at[slot])
        copy = send_tile(tiles.at[slot], out, i, sems.at[slot])
        copy.start()
        copies.append(copy)

    inner_layers(
        g_lo, field_in, g_hi, old, hid, gb, load, bufs, wide, w.at[1], w.at[0], near_out, finish, ends_a
    )
    lons = total // LANES
    ends_b[0] = gate_rows(wide, 0, CHUNK, channels).astype(BF16)
    ends_b[1] = gate_rows(wide, lons - CHUNK, CHUNK, channels).astype(BF16)
    copies[-2].wait()
    copies[-1].wait()


def last(hid_in, field_in, hid_edge, g_lo, g_hi, grad, enc, gates, w, out_shape):
    channels, lons, lats = gates.shape[1:]
    total = lons * lats
    cols = CHUNK * LANES
    levels = enc.shape[0]
    sd = jax.ShapeDtypeStruct
    return pl.pallas_call(
        last_kernel,
        in_specs=[VMEM] * 7 + [HBM, VMEM],
        out_specs=(HBM, VMEM, VMEM, VMEM),
        out_shape=(
            sd(out_shape, F32),
            sd((2, channels, cols), F32),
            sd((2, channels, DIL * LANES), BF16),
            sd((2, channels, cols), BF16),
        ),
        scratch_shapes=[
            pltpu.VMEM((channels, total), F32),
            pltpu.VMEM((channels, total), BF16),
            pltpu.VMEM((2, levels * CHUNK, LANES), F32),
            pltpu.SemaphoreType.DMA((2,)),
        ]
        + gates_scratch(gates),
        compiler_params=params(40),
        name="last",
    )(hid_in, field_in, hid_edge, g_lo, g_hi, grad, enc, gates, w)


def edge_values(which, hid, g_lo, g_hi, halo_lo, halo_hi, near, gate_a, gate_b, ah_lo, ah_hi, w):
    cols = CHUNK * LANES
    step = DIL * LANES
    wa, wb = w.at[2 * which + 1], w.at[2 * which]
    result = []
    for side in range(2):
        if side == 0:
            field = jnp.concatenate([halo_lo[...], g_lo[...]], axis=1)
            old = jnp.concatenate([halo_lo[:, step:].astype(F32), hid[0, :, :step]], axis=1)
            gate = jnp.concatenate([ah_lo[which], gate_a[0]], axis=1)
        else:
            field = jnp.concatenate([g_hi[...], halo_hi[...]], axis=1)
            old = jnp.concatenate([hid[1, :, step:], halo_hi[:, :step].astype(F32)], axis=1)
            gate = jnp.concatenate([gate_a[1], ah_hi[which]], axis=1)
        back = conv(wa, [field[:, d : d + cols] for d in (2 * step, step, 0)])
        new = old + gate.astype(F32) * back
        pieces = (new, near[0]) if side == 0 else (near[1], new)
        joined = jnp.concatenate(pieces, axis=1)
        field = joined.astype(BF16)
        back = conv(wb, [field[:, d : d + cols] for d in (2 * step, step, 0)])
        result.append(joined[:, step : step + cols] + gate_b[side].astype(F32) * back)
    return result


def edge_kernel(which, *refs):
    ins, (hid_out, lo_out, hi_out) = refs[:11], refs[11:]
    lo, hi = edge_values(which, *ins)
    hid_out[0] = lo
    hid_out[1] = hi
    lo_out[...] = lo.astype(BF16)
    hi_out[...] = hi.astype(BF16)


def edge_last_kernel(which, *refs):
    ins, (grad, enc, _), (out, tiles, sems) = refs[:11], refs[11:14], refs[14:]
    levels = enc.shape[0]
    values = edge_values(which, *ins)
    chunks = out.shape[1] // CHUNK
    copies = []
    for side in range(2):
        part = grad[side * levels : (side + 1) * levels, :]
        emit(enc[...], part, values[side], tiles.at[side])
        copy = send_tile(tiles.at[side], out, side * (chunks - 1), sems.at[side])
        copy.start()
        copies.append(copy)
    for copy in copies:
        copy.wait()


def edge(which, *args):
    sd = jax.ShapeDtypeStruct
    hid, g_lo = args[:2]
    return pl.pallas_call(
        functools.partial(edge_kernel, which),
        in_specs=[VMEM] * 11,
        out_specs=(VMEM,) * 3,
        out_shape=(sd(hid.shape, F32), sd(g_lo.shape, BF16), sd(g_lo.shape, BF16)),
        compiler_params=params(18),
        name="edge",
    )(*args)


def edge_last(which, *args):
    enc, state = args[12:]
    return pl.pallas_call(
        functools.partial(edge_last_kernel, which),
        in_specs=[VMEM] * 13 + [HBM],
        out_specs=HBM,
        out_shape=jax.ShapeDtypeStruct(state.shape, F32),
        scratch_shapes=[
            pltpu.VMEM((2, enc.shape[0] * CHUNK, LANES), F32),
            pltpu.SemaphoreType.DMA((2,)),
        ],
        input_output_aliases={13: 0},
        compiler_params=params(18),
        name="edge_last",
    )(*args)


def halos(lo, hi):
    count = lax.axis_size("lon")
    up = [(i, (i + 1) % count) for i in range(count)]
    down = [(b, a) for a, b in up]
    return lax.ppermute(hi, "lon", up), lax.ppermute(lo, "lon", down)


def per_device(resid, index, count, weight, jacobian, decoder, conv_weight, gates, encoder):
    dests = lax.axis_size("lat") * lax.axis_size("lon")
    packed = pack(resid, index, count, weight.reshape(1, -1), dests)
    packed = lax.all_to_all(packed, ("lat", "lon"), split_axis=0, concat_axis=0, tiled=True)
    gate_lo, gate_hi = gate_edges(gates)
    gh_lo, gh_hi = halos(gate_lo, gate_hi)
    jac, dec, enc, w = prepare(jacobian, decoder, encoder, conv_weight, gate_lo)
    incr, key, group, grad_e, hid_e, g_lo, g_hi = front(packed, jac, dec)
    halo_lo, halo_hi = halos(g_lo, g_hi)
    grad_i, hid_i, field_i, near, end_a, end_b = mid(
        incr, key, group, hid_e, g_lo, g_hi, dec, gates, w
    )
    hid_e, g_lo, g_hi = edge(
        1, hid_e, g_lo, g_hi, halo_lo, halo_hi, near, end_a, end_b, gh_lo, gh_hi, w
    )
    halo_lo, halo_hi = halos(g_lo, g_hi)
    out_shape = (jacobian.shape[2],) + gates.shape[2:]
    state, near, end_a, end_b = last(
        hid_i, field_i, hid_e, g_lo, g_hi, grad_i, enc, gates, w, out_shape
    )
    return edge_last(
        0, hid_e, g_lo, g_hi, halo_lo, halo_hi, near, end_a, end_b, gh_lo, gh_hi, w,
        grad_e, enc, state,
    )


def solution(mesh):
    return jax.shard_map(
        per_device,
        mesh=mesh,
        in_specs=(
            P(None, ("lat", "lon")),
            P(None, ("lat", "lon")),
            P(None, ("lat", "lon")),
            P(),
            P(),
            P(),
            P(),
            P(None, None, "lon", "lat"),
            P(),
        ),
        out_specs=P(None, "lon", "lat"),
        check_vma=False,
    )
```

```python
import functools

import jax
import jax.numpy as jnp
from jax import lax
from jax.experimental import pallas as pl
from jax.experimental.pallas import tpu as pltpu
from jax.sharding import PartitionSpec as P


F32 = jnp.float32
BF16 = jnp.bfloat16
LANES = 128
CHUNK = 8
DIL = 4
UNUSED = 255.0


def params(mib):
    return pltpu.CompilerParams(vmem_limit_bytes=mib << 20)


def iota(shape, dim):
    return lax.broadcasted_iota(jnp.int32, shape, dim)


def dot(a, b):
    return jnp.dot(a, b, preferred_element_type=F32)


def pack_kernel(resid_hbm, index_hbm, count_hbm, weight_hbm, out_hbm, resid, index, count, weight, out, in_sems, out_sems):
    parts, dests = out.shape[:2]
    slots = resid.shape[2]
    per = slots // dests
    pairs = per // 2
    small = [
        pltpu.make_async_copy(index_hbm, index, in_sems.at[parts]),
        pltpu.make_async_copy(count_hbm, count, in_sems.at[parts + 1]),
        pltpu.make_async_copy(weight_hbm, weight, in_sems.at[parts + 2]),
    ]
    for copy in small:
        copy.start()
    large = []
    for p in range(parts):
        src = resid_hbm.at[:, p * slots : (p + 1) * slots]
        large.append(pltpu.make_async_copy(src, resid.at[p], in_sems.at[p]))
        large[-1].start()
    width = LANES // pairs
    row = iota((LANES, slots), 0) & (width - 1)
    lane, slot = iota((LANES, slots), 0), iota((LANES, slots), 1)
    mine = ((slot & (per - 1)) >> 1) == (lane >> (width.bit_length() - 1))
    shift = per.bit_length() - 1
    fold_to, fold_from = iota((2 * dests, slots), 0), iota((2 * dests, slots), 1)
    fold = ((fold_from >> shift) * 2 + (fold_from & 1)) == fold_to
    fold = fold.astype(F32).astype(BF16)
    own = (iota((dests, slots), 1) >> shift) == iota((dests, slots), 0)
    own = own.astype(F32).astype(BF16)
    place = (iota((1, slots), 1) & (per - 1)).astype(F32)
    total = dests * parts
    for copy in small:
        copy.wait()
    scale = jnp.broadcast_to(weight[...], (LANES, LANES)).T
    scale = jnp.concatenate([scale] * (slots // LANES), axis=1)
    counts = jnp.broadcast_to(count[...].astype(F32), (8, total)).astype(BF16)
    for copy in large:
        copy.wait()
    sends = []
    for p in range(parts):
        at = slice(p * slots, (p + 1) * slots)
        used = dot(counts[:, p * dests : (p + 1) * dests], own)[0:1]
        cell = index[0:1, at]
        kind = index[1:2, at].astype(F32)
        valid = place < used
        low = ((cell >> 7) & (CHUNK - 1)).astype(F32)
        lat = (cell & (LANES - 1)).astype(F32)
        group = jnp.where(valid, (cell >> 10).astype(F32), UNUSED)
        meta = jnp.where(row == 0, low, jnp.where(row == 1, lat, jnp.where(row == 2, group, kind)))
        meta = jnp.where(mine, meta, 0.0).astype(BF16)
        meta = lax.dot_general(fold, meta, (((1,), (1,)), ((), ())), preferred_element_type=F32)
        out[p, :, pairs : pairs + 1] = meta.astype(BF16).reshape(dests, 1, 2, LANES)
        weighted = scale * resid[p].astype(F32)
        out[p, :, 0:pairs] = weighted.astype(BF16).T.reshape(dests, pairs, 2, LANES)
    for p in range(parts):
        dst = out_hbm.at[p * dests : (p + 1) * dests]
        sends.append(pltpu.make_async_copy(out.at[p], dst, out_sems.at[p]))
        sends[-1].start()
    for copy in sends:
        copy.wait()


HBM = pl.BlockSpec(memory_space=pltpu.HBM)
VMEM = pl.BlockSpec(memory_space=pltpu.VMEM)
ANY = pl.BlockSpec(memory_space=pl.ANY)
SMEM = pl.BlockSpec(memory_space=pltpu.SMEM)


def by_side(odd, far_side, body):
    for parity in range(2):
        side = parity if far_side else 1 - parity

        @pl.when(odd[0] == parity)
        def _(side=side):
            body(side)


def pack(resid, index, count, weight, dests):
    channels, slots = resid.shape
    per = slots // dests
    parts = 4
    return pl.pallas_call(
        pack_kernel,
        in_specs=[HBM] * 4,
        out_specs=HBM,
        out_shape=jax.ShapeDtypeStruct((dests, per // 2 + 1, 2, LANES), BF16),
        scratch_shapes=[
            pltpu.VMEM((parts, channels, slots // parts), BF16),
            pltpu.VMEM(index.shape, jnp.int32),
            pltpu.VMEM(count.shape, jnp.int32),
            pltpu.VMEM(weight.shape, F32),
            pltpu.VMEM((parts, dests // parts, per // 2 + 1, 2, LANES), BF16),
            pltpu.SemaphoreType.DMA((parts + 3,)),
            pltpu.SemaphoreType.DMA((parts,)),
        ],
        compiler_params=params(63),
        name="pack",
    )(resid, index, count, weight)


def by_channel(wide, lon, pitch, c):
    a = wide[pl.ds(c * pitch + lon, 8, stride=pitch), :]
    b = wide[pl.ds((c + 8) * pitch + lon, 8, stride=pitch), :]
    return jnp.concatenate([a, b], axis=0).astype(BF16)


def prepare_kernel(jac, dec, enc, conv_w, after, jac_out, dec_out, enc_out, w_out, rows, tall):
    del after
    levels, kinds = jac.shape[:2]
    padded = enc_out.shape[0]
    rows[...] = jnp.zeros_like(rows)
    rows[0 : levels * kinds, :] = jac[...].astype(F32).reshape(levels * kinds, LANES)
    for k in range(kinds):
        for l in range(0, padded, 16):
            jac_out[l : l + 16, k * LANES : (k + 1) * LANES] = by_channel(rows, k, kinds, l)
    tall[...] = jnp.zeros_like(tall)
    tall[0:levels, :] = enc[...].astype(F32)
    enc_out[...] = tall[0:padded, :].astype(BF16)
    tall[0:levels, :] = dec[...].astype(F32)
    dec_out[...] = tall[...].T[:, 0:padded].astype(BF16)
    for layer in range(conv_w.shape[0]):
        w_out[layer] = conv_w[layer].T


def prepare(jacobian, decoder, encoder, conv_weight, after):
    channels, kinds, levels = jacobian.shape
    layers = conv_weight.shape[0]
    padded = levels + -levels % 16
    conv_w = conv_weight.reshape(layers, -1, channels)
    sd = jax.ShapeDtypeStruct
    return pl.pallas_call(
        prepare_kernel,
        in_specs=[VMEM] * 4 + [ANY],
        out_specs=(VMEM,) * 4,
        out_shape=(
            sd((padded, kinds * channels), BF16),
            sd((channels, padded), BF16),
            sd((padded, channels), BF16),
            sd((layers, channels, conv_w.shape[1]), BF16),
        ),
        scratch_shapes=[
            pltpu.VMEM((padded * kinds, channels), F32),
            pltpu.VMEM((256, channels), F32),
        ],
        compiler_params=params(20),
        name="prepare",
    )(jacobian.transpose(2, 1, 0), decoder, encoder.T, conv_w, after)


def gate_edges_kernel(odd, src, far, close, both, buf, wide, sems):
    channels, lons, lats = src.shape[1:]
    copies = []
    for k in range(2):
        for side in range(2):
            at = side * (lons - CHUNK)
            part = src.at[2 * k + 1, :, at : at + CHUNK, :]
            copies.append(pltpu.make_async_copy(part, buf.at[k, side], sems.at[k, side]))
            copies[-1].start()
    for k in range(2):
        for side in range(2):
            copies[2 * k + side].wait()
            wide[k, side] = buf[k, side].astype(F32).reshape(channels * CHUNK, lats)
            for r in range(DIL):
                for c in range(0, channels, 16):
                    value = by_channel(wide.at[k, side], side * DIL + r, CHUNK, c)
                    both[side, k, c : c + 16, r * lats : (r + 1) * lats] = value

    def split(side):
        far[...] = both[side]
        close[...] = both[1 - side]

    by_side(odd, True, split)


def gate_edges(odd, gates):
    _, channels, _, lats = gates.shape
    send = jax.ShapeDtypeStruct((2, channels, DIL * lats), BF16)
    return pl.pallas_call(
        gate_edges_kernel,
        in_specs=[SMEM, HBM],
        out_specs=(VMEM,) * 2,
        out_shape=(send,) * 2,
        scratch_shapes=[
            pltpu.VMEM((2, 2, channels, DIL * lats), BF16),
            pltpu.VMEM((2, 2, channels, CHUNK, lats), BF16),
            pltpu.VMEM((2, 2, channels * CHUNK, lats), F32),
            pltpu.SemaphoreType.DMA((2, 2)),
        ],
        compiler_params=params(58),
        name="gate_edges",
    )(odd, gates)


def front_kernel(
    odd, packed, jac, dec,
    incr_out, key_out, group_out, grad_out, hid_out, lo_out, hi_out, far_out, close_out,
):
    senders, pairs = packed.shape[0], packed.shape[1] - 1
    part = 2 * senders
    slots = pairs * part
    width = LANES // pairs
    levels = jac.shape[0]
    kinds = jac.shape[1] // LANES
    x = jnp.concatenate([packed[:, m].reshape(part, LANES).T for m in range(pairs)], axis=1)
    meta = packed[:, pairs].reshape(part, LANES)
    meta_t = meta.astype(F32).T

    def line(q):
        rows = [m * width + q for m in range(pairs)]
        return jnp.concatenate([meta_t[r : r + 1] for r in rows], axis=1)

    def place(m):
        source = iota((LANES, LANES), 0) - m * width
        pick = jnp.where(source == 0, float(LANES), jnp.where(source == 1, 1.0, 0.0))
        return dot(meta, pick.astype(BF16))

    group = line(2)
    kind = line(3)
    group_out[...] = jnp.broadcast_to(group, (8, slots))
    spread = jnp.concatenate(
        [x * (kind == k).astype(F32).astype(BF16) for k in range(kinds)], axis=0
    )
    incr = dot(jac[...], spread).astype(BF16)
    incr_out[...] = incr
    key = jnp.concatenate([place(m) for m in range(pairs)], axis=0)
    key = key - iota((slots, LANES), 1).astype(F32)
    key_out[...] = key
    onehot = hot(key)
    last = CHUNK - 1
    lhs = jnp.concatenate(
        [incr * (group == g).astype(F32).astype(BF16) for g in (0, last)], axis=0
    )
    grad = dot(lhs, onehot)
    grad_out[...] = grad
    for side in range(2):
        part = grad[side * levels : (side + 1) * levels].astype(BF16)
        hidden = dot(dec[...], part)
        hid_out[side] = hidden
        (lo_out, hi_out)[side][...] = hidden.astype(BF16)

    def split(side):
        far_out[...] = (lo_out, hi_out)[side][...]
        close_out[...] = (hi_out, lo_out)[side][...]

    by_side(odd, True, split)


def hot(key):
    return jnp.concatenate(
        [jnp.where(key == float(r * LANES), 1.0, 0.0).astype(BF16) for r in range(CHUNK)], axis=1
    )


def front(odd, packed, jac, dec):
    slots = packed.shape[0] * (packed.shape[1] - 1) * 2
    levels = jac.shape[0]
    cols = CHUNK * LANES
    sd = jax.ShapeDtypeStruct
    return pl.pallas_call(
        front_kernel,
        in_specs=[SMEM] + [VMEM] * 3,
        out_specs=(VMEM,) * 9,
        out_shape=(
            sd((levels, slots), BF16),
            sd((slots, LANES), F32),
            sd((8, slots), F32),
            sd((2 * levels, cols), F32),
            sd((2, LANES, cols), F32),
            sd((LANES, cols), BF16),
            sd((LANES, cols), BF16),
            sd((LANES, cols), BF16),
            sd((LANES, cols), BF16),
        ),
        compiler_params=params(28),
        name="front",
    )(odd, packed, jac, dec)


def conv(weight, taps):
    return dot(weight[...], jnp.concatenate(taps, axis=0))


def pieces(low, inside, high, start, size):
    parts = []
    at = 0
    for ref in (low, inside, high):
        first, stop = max(start - at, 0), min(start + size - at, ref.shape[1])
        if first < stop:
            parts.append(ref[:, first:stop])
        at += ref.shape[1]
    return parts[0] if len(parts) == 1 else jnp.concatenate(parts, axis=1)


def load_gates(gates, layer, bufs, sems):
    copies = [
        pltpu.make_async_copy(gates.at[layer - i], bufs.at[i], sems.at[i]) for i in range(2)
    ]
    for copy in copies:
        copy.start()
    return copies


def widen(copy, buf, wide):
    channels, lons = buf.shape[:2]
    pitch = wide.shape[0] // channels
    copy.wait()

    def body(c, carry):
        wide[pl.ds(pl.multiple_of(c * pitch, 8), lons), :] = buf[c].astype(F32)
        return carry

    lax.fori_loop(0, channels, body, 0, unroll=8)


def gate_rows(wide, lon, count, channels):
    pitch = wide.shape[0] // channels
    columns = [
        jnp.concatenate(
            [wide[pl.ds(c * pitch + r, 8, stride=pitch), :] for c in range(0, channels, 8)], axis=0
        )
        for r in range(lon, lon + count)
    ]
    return jnp.concatenate(columns, axis=1)


def inner_layers(low, inside, high, old, hid, gb, load, bufs, wide, wa, wb, near_out, finish, ends=None):
    cols = CHUNK * LANES
    step = DIL * LANES
    channels, total = hid.shape
    count = total // cols
    widen(load[0], bufs.at[0], wide)
    for i in range(count - 1):
        o = step + i * cols
        at = slice(o, o + cols)
        taps = [pieces(low, inside, high, o + d, cols) for d in (step, 0, -step)]
        back = conv(wa, taps)
        new = old(o, cols) + gate_rows(wide, o // LANES, CHUNK, channels) * back
        hid[:, at] = new
        gb[:, at] = new.astype(BF16)
    near_out[0] = hid[:, step : step + cols]
    near_out[1] = hid[:, total - step - cols : total - step]
    lons = total // LANES
    if ends is not None:
        ends[0] = gate_rows(wide, 0, DIL, channels).astype(BF16)
        ends[1] = gate_rows(wide, lons - DIL, DIL, channels).astype(BF16)
    widen(load[1], bufs.at[1], wide)
    for i in range(1, count - 1):
        o = i * cols
        at = slice(o, o + cols)
        back = conv(wb, [gb[:, o + d : o + d + cols] for d in (step, 0, -step)])
        finish(i, hid[:, at] + gate_rows(wide, o // LANES, CHUNK, channels) * back)


def mid_kernel(
    incr, key, group, hid_edge, g_lo, g_hi, dec, gates, w,
    grad_out, hid_out, field_out, near_out, ends_a, ends_b,
    hid, ga, gb, lhs, onehot, bufs, wide, sems,
):
    load = load_gates(gates, 3, bufs, sems)
    cols = CHUNK * LANES
    levels = incr.shape[0]
    channels, total = hid.shape
    inner = total // cols - 2
    onehot[...] = hot(key[...])
    for g in range(inner):
        mask = (group[0:1, :] == float(g + 1)).astype(F32).astype(BF16)
        lhs[g * levels : (g + 1) * levels, :] = incr[...] * mask
    hid[:, 0:cols] = hid_edge[0]
    hid[:, total - cols : total] = hid_edge[1]
    for n in range(0, cols, 256):
        grad_out[:, n : n + 256] = dot(lhs[...], onehot[:, n : n + 256])
    for g in range(inner):
        new = dot(dec[...], grad_out[g * levels : (g + 1) * levels, :].astype(BF16))
        hid[:, (g + 1) * cols : (g + 2) * cols] = new
        ga[:, g * cols : (g + 1) * cols] = new.astype(BF16)

    def old(o, size):
        return hid[:, o : o + size]

    def finish(i, value):
        hid_out[:, (i - 1) * cols : i * cols] = value
        field_out[:, (i - 1) * cols : i * cols] = value.astype(BF16)

    inner_layers(
        g_lo, ga, g_hi, old, hid, gb, load, bufs, wide, w.at[3], w.at[2], near_out, finish, ends_a
    )
    lons = total // LANES
    ends_b[0] = gate_rows(wide, 0, CHUNK, channels).astype(BF16)
    ends_b[1] = gate_rows(wide, lons - CHUNK, CHUNK, channels).astype(BF16)


def gates_scratch(gates):
    channels, lons, lats = gates.shape[1:]
    return [
        pltpu.VMEM((2, channels, lons, lats), BF16),
        pltpu.VMEM((channels * (lons + 8), lats), F32),
        pltpu.SemaphoreType.DMA((2,)),
    ]


def mid(incr, key, group, hid_edge, g_lo, g_hi, dec, gates, w):
    levels, slots = incr.shape
    channels, lons, lats = gates.shape[1:]
    total = lons * lats
    cols = CHUNK * LANES
    inner = total // cols - 2
    sd = jax.ShapeDtypeStruct
    outs = (
        sd((inner * levels, cols), F32),
        sd((channels, inner * cols), F32),
        sd((channels, inner * cols), BF16),
        sd((2, channels, cols), F32),
        sd((2, channels, DIL * LANES), BF16),
        sd((2, channels, cols), BF16),
    )
    return pl.pallas_call(
        mid_kernel,
        in_specs=[VMEM] * 7 + [HBM, VMEM],
        out_specs=(VMEM,) * 6,
        out_shape=outs,
        scratch_shapes=[
            pltpu.VMEM((channels, total), F32),
            pltpu.VMEM((channels, inner * cols), BF16),
            pltpu.VMEM((channels, total), BF16),
            pltpu.VMEM((inner * levels, slots), BF16),
            pltpu.VMEM((slots, cols), BF16),
        ]
        + gates_scratch(gates),
        compiler_params=params(40),
        name="mid",
    )(incr, key, group, hid_edge, g_lo, g_hi, dec, gates, w)


def emit(enc, grad, value, tile):
    full = grad + dot(enc, value.astype(BF16))
    for r in range(CHUNK):
        for l in range(0, full.shape[0], 8):
            tile[pl.ds(l * CHUNK + r, 8, stride=CHUNK), :] = full[
                l : l + 8, r * LANES : (r + 1) * LANES
            ]


def send_tile(tile, out, chunk, sem):
    levels = out.shape[0]
    src = tile.reshape(tile.shape[0] // CHUNK, CHUNK, LANES)
    return pltpu.make_async_copy(
        src.at[0:levels], out.at[:, CHUNK * chunk : CHUNK * (chunk + 1), :], sem
    )


def last_kernel(
    hid_in, field_in, hid_edge, g_lo, g_hi, grad, enc, gates, w,
    out, near_out, ends_a, ends_b, hid, gb, tiles, sems, bufs, wide, gate_sems,
):
    load = load_gates(gates, 1, bufs, gate_sems)
    channels, total = hid.shape
    levels = enc.shape[0]
    copies = []

    def old(o, size):
        return pieces(hid_edge.at[0], hid_in, hid_edge.at[1], o, size)

    def finish(i, value):
        slot = (i - 1) % 2
        if i > 2:
            copies[i - 3].wait()
        emit(enc[...], grad[(i - 1) * levels : i * levels, :], value, tiles.at[slot])
        copy = send_tile(tiles.at[slot], out, i, sems.at[slot])
        copy.start()
        copies.append(copy)

    inner_layers(
        g_lo, field_in, g_hi, old, hid, gb, load, bufs, wide, w.at[1], w.at[0], near_out, finish, ends_a
    )
    lons = total // LANES
    ends_b[0] = gate_rows(wide, 0, CHUNK, channels).astype(BF16)
    ends_b[1] = gate_rows(wide, lons - CHUNK, CHUNK, channels).astype(BF16)
    copies[-2].wait()
    copies[-1].wait()


def last(hid_in, field_in, hid_edge, g_lo, g_hi, grad, enc, gates, w, out_shape):
    channels, lons, lats = gates.shape[1:]
    total = lons * lats
    cols = CHUNK * LANES
    levels = enc.shape[0]
    sd = jax.ShapeDtypeStruct
    return pl.pallas_call(
        last_kernel,
        in_specs=[VMEM] * 7 + [HBM, VMEM],
        out_specs=(HBM, VMEM, VMEM, VMEM),
        out_shape=(
            sd(out_shape, F32),
            sd((2, channels, cols), F32),
            sd((2, channels, DIL * LANES), BF16),
            sd((2, channels, cols), BF16),
        ),
        scratch_shapes=[
            pltpu.VMEM((channels, total), F32),
            pltpu.VMEM((channels, total), BF16),
            pltpu.VMEM((2, levels * CHUNK, LANES), F32),
            pltpu.SemaphoreType.DMA((2,)),
        ]
        + gates_scratch(gates),
        compiler_params=params(40),
        name="last",
    )(hid_in, field_in, hid_edge, g_lo, g_hi, grad, enc, gates, w)


def edge_value(which, side, hid, g_lo, g_hi, halo, near, gate_a, gate_b, gate_halo, w):
    cols = CHUNK * LANES
    step = DIL * LANES
    wa, wb = w.at[2 * which + 1], w.at[2 * which]
    if side == 0:
        field = jnp.concatenate([halo[...], g_lo[...]], axis=1)
        old = jnp.concatenate([halo[:, step:].astype(F32), hid[0, :, :step]], axis=1)
        gate = jnp.concatenate([gate_halo[which], gate_a[0]], axis=1)
    else:
        field = jnp.concatenate([g_hi[...], halo[...]], axis=1)
        old = jnp.concatenate([hid[1, :, step:], halo[:, :step].astype(F32)], axis=1)
        gate = jnp.concatenate([gate_a[1], gate_halo[which]], axis=1)
    back = conv(wa, [field[:, d : d + cols] for d in (2 * step, step, 0)])
    new = old + gate.astype(F32) * back
    joined = jnp.concatenate((new, near[0]) if side == 0 else (near[1], new), axis=1)
    field = joined.astype(BF16)
    back = conv(wb, [field[:, d : d + cols] for d in (2 * step, step, 0)])
    return joined[:, step : step + cols] + gate_b[side].astype(F32) * back


def edge_far_kernel(which, odd, *refs):
    ins, (hid_out, send) = refs[:9], refs[9:]

    def body(side):
        value = edge_value(which, side, *ins)
        hid_out[...] = value
        send[...] = value.astype(BF16)

    by_side(odd, True, body)


def edge_close_kernel(which, odd, *refs):
    ins, (far_hid, far_g), (hid_out, lo_out, hi_out, send) = refs[:9], refs[9:11], refs[11:]

    def body(side):
        value = edge_value(which, side, *ins)
        hid_out[side] = value
        send[...] = value.astype(BF16)
        (lo_out, hi_out)[side][...] = value.astype(BF16)
        hid_out[1 - side] = far_hid[...]
        (hi_out, lo_out)[side][...] = far_g[...]

    by_side(odd, False, body)


def edge_last_kernel(which, far_side, odd, *refs):
    ins, (grad, enc, _), (out, tile, sem) = refs[:9], refs[9:12], refs[12:]
    levels = enc.shape[0]
    chunks = out.shape[1] // CHUNK

    def body(side):
        value = edge_value(which, side, *ins)
        emit(enc[...], grad[side * levels : (side + 1) * levels, :], value, tile)
        copy = send_tile(tile, out, side * (chunks - 1), sem)
        copy.start()
        copy.wait()

    by_side(odd, far_side, body)


def edge_far(which, *args):
    sd = jax.ShapeDtypeStruct
    g_lo = args[2]
    return pl.pallas_call(
        functools.partial(edge_far_kernel, which),
        in_specs=[SMEM] + [VMEM] * 9,
        out_specs=(VMEM,) * 2,
        out_shape=(sd(g_lo.shape, F32), sd(g_lo.shape, BF16)),
        compiler_params=params(18),
        name="edge_far",
    )(*args)


def edge_close(which, *args):
    sd = jax.ShapeDtypeStruct
    hid, g_lo = args[1:3]
    return pl.pallas_call(
        functools.partial(edge_close_kernel, which),
        in_specs=[SMEM] + [VMEM] * 11,
        out_specs=(VMEM,) * 4,
        out_shape=(sd(hid.shape, F32),) + (sd(g_lo.shape, BF16),) * 3,
        compiler_params=params(18),
        name="edge_close",
    )(*args)


def edge_last(which, far_side, *args):
    enc, state = args[-2:]
    return pl.pallas_call(
        functools.partial(edge_last_kernel, which, far_side),
        in_specs=[SMEM] + [VMEM] * 11 + [HBM],
        out_specs=HBM,
        out_shape=jax.ShapeDtypeStruct(state.shape, F32),
        scratch_shapes=[
            pltpu.VMEM((enc.shape[0] * CHUNK, LANES), F32),
            pltpu.SemaphoreType.DMA,
        ],
        input_output_aliases={12: 0},
        compiler_params=params(18),
        name="edge_last",
    )(*args)


def swap(value, first):
    count = lax.axis_size("lon")
    pairs = []
    for i in range(first, first + count, 2):
        low, high = i % count, (i + 1) % count
        pairs += [(low, high), (high, low)]
    return lax.ppermute(value, "lon", pairs)


def program(resid, index, count, weight, jacobian, decoder, conv_weight, gates, encoder):
    dests = lax.axis_size("lat") * lax.axis_size("lon")
    odd = (lax.axis_index("lon") % 2).astype(jnp.int32).reshape(1)
    packed = pack(resid, index, count, weight.reshape(1, -1), dests)
    packed = lax.all_to_all(packed, ("lat", "lon"), split_axis=0, concat_axis=0, tiled=True)
    gate_far, gate_close = gate_edges(odd, gates)
    gate_far_halo = swap(gate_far, 1)
    gate_close_halo = swap(gate_close, 0)
    jac, dec, enc, w = prepare(jacobian, decoder, encoder, conv_weight, gate_far)
    incr, key, group, grad_e, hid_e, g_lo, g_hi, far, close = front(odd, packed, jac, dec)
    far = swap(far, 1)
    close = swap(close, 0)
    grad_i, hid_i, field_i, near, end_a, end_b = mid(
        incr, key, group, hid_e, g_lo, g_hi, dec, gates, w
    )
    far_hid, far_g = edge_far(1, odd, hid_e, g_lo, g_hi, far, near, end_a, end_b, gate_far_halo, w)
    far = swap(far_g, 1)
    hid_e, g_lo, g_hi, close = edge_close(
        1, odd, hid_e, g_lo, g_hi, close, near, end_a, end_b, gate_close_halo, w, far_hid, far_g
    )
    close = swap(close, 0)
    out_shape = (jacobian.shape[2],) + gates.shape[2:]
    state, near, end_a, end_b = last(
        hid_i, field_i, hid_e, g_lo, g_hi, grad_i, enc, gates, w, out_shape
    )
    halves = ((FAR_FIRST, far, gate_far_halo), (not FAR_FIRST, close, gate_close_halo))
    if not FAR_FIRST:
        halves = ((False, close, gate_close_halo), (True, far, gate_far_halo))
    for far_side, halo, gate_halo in halves:
        state = edge_last(
            0, far_side, odd, hid_e, g_lo, g_hi, halo, near, end_a, end_b, gate_halo, w,
            grad_e, enc, state,
        )
    return state


FAR_FIRST = True


def solution(mesh):
    return jax.shard_map(
        program,
        mesh=mesh,
        in_specs=(
            P(None, ("lat", "lon")),
            P(None, ("lat", "lon")),
            P(None, ("lat", "lon")),
            P(),
            P(),
            P(),
            P(),
            P(None, None, "lon", "lat"),
            P(),
        ),
        out_specs=P(None, "lon", "lat"),
        check_vma=False,
    )
```

```python
import functools

import jax
import jax.numpy as jnp
from jax import lax
from jax.experimental import pallas as pl
from jax.experimental.pallas import tpu as pltpu
from jax.sharding import PartitionSpec as P


F32 = jnp.float32
BF16 = jnp.bfloat16
LANES = 128
CHUNK = 8
DIL = 4
UNUSED = 255.0


def params(mib):
    return pltpu.CompilerParams(vmem_limit_bytes=mib << 20)


def iota(shape, dim):
    return lax.broadcasted_iota(jnp.int32, shape, dim)


def dot(a, b):
    return jnp.dot(a, b, preferred_element_type=F32)


def pack_kernel(resid_hbm, index_hbm, count_hbm, weight_hbm, out_hbm, resid, index, count, weight, out, in_sems, out_sems):
    parts, dests = out.shape[:2]
    slots = resid.shape[2]
    per = slots // dests
    pairs = per // 2
    small = [
        pltpu.make_async_copy(index_hbm, index, in_sems.at[parts]),
        pltpu.make_async_copy(count_hbm, count, in_sems.at[parts + 1]),
        pltpu.make_async_copy(weight_hbm, weight, in_sems.at[parts + 2]),
    ]
    for copy in small:
        copy.start()
    large = []
    for p in range(parts):
        src = resid_hbm.at[:, p * slots : (p + 1) * slots]
        large.append(pltpu.make_async_copy(src, resid.at[p], in_sems.at[p]))
        large[-1].start()
    width = LANES // pairs
    row = iota((LANES, slots), 0) & (width - 1)
    lane, slot = iota((LANES, slots), 0), iota((LANES, slots), 1)
    mine = ((slot & (per - 1)) >> 1) == (lane >> (width.bit_length() - 1))
    shift = per.bit_length() - 1
    fold_to, fold_from = iota((2 * dests, slots), 0), iota((2 * dests, slots), 1)
    fold = ((fold_from >> shift) * 2 + (fold_from & 1)) == fold_to
    fold = fold.astype(F32).astype(BF16)
    own = (iota((dests, slots), 1) >> shift) == iota((dests, slots), 0)
    own = own.astype(F32).astype(BF16)
    place = (iota((1, slots), 1) & (per - 1)).astype(F32)
    total = dests * parts
    for copy in small:
        copy.wait()
    scale = jnp.broadcast_to(weight[...], (LANES, LANES)).T
    scale = jnp.concatenate([scale] * (slots // LANES), axis=1)
    counts = jnp.broadcast_to(count[...].astype(F32), (8, total)).astype(BF16)
    for copy in large:
        copy.wait()
    sends = []
    for p in range(parts):
        at = slice(p * slots, (p + 1) * slots)
        used = dot(counts[:, p * dests : (p + 1) * dests], own)[0:1]
        cell = index[0:1, at]
        kind = index[1:2, at].astype(F32)
        valid = place < used
        low = ((cell >> 7) & (CHUNK - 1)).astype(F32)
        lat = (cell & (LANES - 1)).astype(F32)
        group = jnp.where(valid, (cell >> 10).astype(F32), UNUSED)
        meta = jnp.where(row == 0, low, jnp.where(row == 1, lat, jnp.where(row == 2, group, kind)))
        meta = jnp.where(mine, meta, 0.0).astype(BF16)
        meta = lax.dot_general(fold, meta, (((1,), (1,)), ((), ())), preferred_element_type=F32)
        out[p, :, pairs : pairs + 1] = meta.astype(BF16).reshape(dests, 1, 2, LANES)
        weighted = scale * resid[p].astype(F32)
        out[p, :, 0:pairs] = weighted.astype(BF16).T.reshape(dests, pairs, 2, LANES)
        dst = out_hbm.at[p * dests : (p + 1) * dests]
        sends.append(pltpu.make_async_copy(out.at[p], dst, out_sems.at[p]))
        sends[-1].start()
    for copy in sends:
        copy.wait()


HBM = pl.BlockSpec(memory_space=pltpu.HBM)
VMEM = pl.BlockSpec(memory_space=pltpu.VMEM)
ANY = pl.BlockSpec(memory_space=pl.ANY)
SMEM = pl.BlockSpec(memory_space=pltpu.SMEM)


def by_side(odd, far_side, body):
    for parity in range(2):
        side = parity if far_side else 1 - parity

        @pl.when(odd[0] == parity)
        def _(side=side):
            body(side)


def pack(resid, index, count, weight, dests):
    channels, slots = resid.shape
    per = slots // dests
    parts = 4
    return pl.pallas_call(
        pack_kernel,
        in_specs=[HBM] * 4,
        out_specs=HBM,
        out_shape=jax.ShapeDtypeStruct((dests, per // 2 + 1, 2, LANES), BF16),
        scratch_shapes=[
            pltpu.VMEM((parts, channels, slots // parts), BF16),
            pltpu.VMEM(index.shape, jnp.int32),
            pltpu.VMEM(count.shape, jnp.int32),
            pltpu.VMEM(weight.shape, F32),
            pltpu.VMEM((parts, dests // parts, per // 2 + 1, 2, LANES), BF16),
            pltpu.SemaphoreType.DMA((parts + 3,)),
            pltpu.SemaphoreType.DMA((parts,)),
        ],
        compiler_params=params(63),
        name="pack",
    )(resid, index, count, weight)


def by_channel(wide, lon, pitch, c):
    a = wide[pl.ds(c * pitch + lon, 8, stride=pitch), :]
    b = wide[pl.ds((c + 8) * pitch + lon, 8, stride=pitch), :]
    return jnp.concatenate([a, b], axis=0).astype(BF16)


def prepare_kernel(jac, dec, enc, conv_w, after, jac_out, dec_out, enc_out, w_out, rows, tall):
    del after
    levels, kinds = jac.shape[:2]
    padded = enc_out.shape[0]
    rows[...] = jnp.zeros_like(rows)
    rows[0 : levels * kinds, :] = jac[...].astype(F32).reshape(levels * kinds, LANES)
    for k in range(kinds):
        for l in range(0, padded, 16):
            jac_out[l : l + 16, k * LANES : (k + 1) * LANES] = by_channel(rows, k, kinds, l)
    tall[...] = jnp.zeros_like(tall)
    tall[0:levels, :] = enc[...].astype(F32)
    enc_out[...] = tall[0:padded, :].astype(BF16)
    tall[0:levels, :] = dec[...].astype(F32)
    dec_out[...] = tall[...].T[:, 0:padded].astype(BF16)
    for layer in range(conv_w.shape[0]):
        w_out[layer] = conv_w[layer].T


def prepare(jacobian, decoder, encoder, conv_weight, after):
    channels, kinds, levels = jacobian.shape
    layers = conv_weight.shape[0]
    padded = levels + -levels % 16
    conv_w = conv_weight.reshape(layers, -1, channels)
    sd = jax.ShapeDtypeStruct
    return pl.pallas_call(
        prepare_kernel,
        in_specs=[VMEM] * 4 + [ANY],
        out_specs=(VMEM,) * 4,
        out_shape=(
            sd((padded, kinds * channels), BF16),
            sd((channels, padded), BF16),
            sd((padded, channels), BF16),
            sd((layers, channels, conv_w.shape[1]), BF16),
        ),
        scratch_shapes=[
            pltpu.VMEM((padded * kinds, channels), F32),
            pltpu.VMEM((256, channels), F32),
        ],
        compiler_params=params(20),
        name="prepare",
    )(jacobian.transpose(2, 1, 0), decoder, encoder.T, conv_w, after)


def gate_edges_kernel(odd, src, far, close, both, buf, wide, sems):
    channels, lons, lats = src.shape[1:]
    copies = []
    for k in range(2):
        for side in range(2):
            at = side * (lons - CHUNK)
            part = src.at[2 * k + 1, :, at : at + CHUNK, :]
            copies.append(pltpu.make_async_copy(part, buf.at[k, side], sems.at[k, side]))
            copies[-1].start()
    for k in range(2):
        for side in range(2):
            copies[2 * k + side].wait()
            wide[k, side] = buf[k, side].astype(F32).reshape(channels * CHUNK, lats)
            for r in range(DIL):
                for c in range(0, channels, 16):
                    value = by_channel(wide.at[k, side], side * DIL + r, CHUNK, c)
                    both[side, k, c : c + 16, r * lats : (r + 1) * lats] = value

    def split(side):
        far[...] = both[side]
        close[...] = both[1 - side]

    by_side(odd, True, split)


def gate_edges(odd, gates):
    _, channels, _, lats = gates.shape
    send = jax.ShapeDtypeStruct((2, channels, DIL * lats), BF16)
    return pl.pallas_call(
        gate_edges_kernel,
        in_specs=[SMEM, HBM],
        out_specs=(VMEM,) * 2,
        out_shape=(send,) * 2,
        scratch_shapes=[
            pltpu.VMEM((2, 2, channels, DIL * lats), BF16),
            pltpu.VMEM((2, 2, channels, CHUNK, lats), BF16),
            pltpu.VMEM((2, 2, channels * CHUNK, lats), F32),
            pltpu.SemaphoreType.DMA((2, 2)),
        ],
        compiler_params=params(58),
        name="gate_edges",
    )(odd, gates)


def front_kernel(
    odd, packed, jac, dec,
    incr_out, key_out, group_out, grad_out, hid_out, lo_out, hi_out, far_out, close_out,
):
    senders, pairs = packed.shape[0], packed.shape[1] - 1
    part = 2 * senders
    slots = pairs * part
    width = LANES // pairs
    levels = jac.shape[0]
    kinds = jac.shape[1] // LANES
    x = jnp.concatenate([packed[:, m].reshape(part, LANES).T for m in range(pairs)], axis=1)
    meta = packed[:, pairs].reshape(part, LANES)
    meta_t = meta.astype(F32).T

    def line(q):
        rows = [m * width + q for m in range(pairs)]
        return jnp.concatenate([meta_t[r : r + 1] for r in rows], axis=1)

    def place(m):
        source = iota((LANES, LANES), 0) - m * width
        pick = jnp.where(source == 0, float(LANES), jnp.where(source == 1, 1.0, 0.0))
        return dot(meta, pick.astype(BF16))

    group = line(2)
    kind = line(3)
    group_out[...] = jnp.broadcast_to(group, (8, slots))
    spread = jnp.concatenate(
        [x * (kind == k).astype(F32).astype(BF16) for k in range(kinds)], axis=0
    )
    incr = dot(jac[...], spread).astype(BF16)
    incr_out[...] = incr
    key = jnp.concatenate([place(m) for m in range(pairs)], axis=0)
    key = key - iota((slots, LANES), 1).astype(F32)
    key_out[...] = key
    onehot = hot(key)
    last = CHUNK - 1
    lhs = jnp.concatenate(
        [incr * (group == g).astype(F32).astype(BF16) for g in (0, last)], axis=0
    )
    grad = dot(lhs, onehot)
    grad_out[...] = grad
    for side in range(2):
        part = grad[side * levels : (side + 1) * levels].astype(BF16)
        hidden = dot(dec[...], part)
        hid_out[side] = hidden
        (lo_out, hi_out)[side][...] = hidden.astype(BF16)

    def split(side):
        far_out[...] = (lo_out, hi_out)[side][...]
        close_out[...] = (hi_out, lo_out)[side][...]

    by_side(odd, True, split)


def hot(key):
    return jnp.concatenate(
        [jnp.where(key == float(r * LANES), 1.0, 0.0).astype(BF16) for r in range(CHUNK)], axis=1
    )


def front(odd, packed, jac, dec):
    slots = packed.shape[0] * (packed.shape[1] - 1) * 2
    levels = jac.shape[0]
    cols = CHUNK * LANES
    sd = jax.ShapeDtypeStruct
    return pl.pallas_call(
        front_kernel,
        in_specs=[SMEM] + [VMEM] * 3,
        out_specs=(VMEM,) * 9,
        out_shape=(
            sd((levels, slots), BF16),
            sd((slots, LANES), F32),
            sd((8, slots), F32),
            sd((2 * levels, cols), F32),
            sd((2, LANES, cols), F32),
            sd((LANES, cols), BF16),
            sd((LANES, cols), BF16),
            sd((LANES, cols), BF16),
            sd((LANES, cols), BF16),
        ),
        compiler_params=params(28),
        name="front",
    )(odd, packed, jac, dec)


def conv(weight, taps):
    return dot(weight[...], jnp.concatenate(taps, axis=0))


def pieces(low, inside, high, start, size):
    parts = []
    at = 0
    for ref in (low, inside, high):
        first, stop = max(start - at, 0), min(start + size - at, ref.shape[1])
        if first < stop:
            parts.append(ref[:, first:stop])
        at += ref.shape[1]
    return parts[0] if len(parts) == 1 else jnp.concatenate(parts, axis=1)


def load_gates(gates, layer, bufs, sems):
    copies = [
        pltpu.make_async_copy(gates.at[layer - i], bufs.at[i], sems.at[i]) for i in range(2)
    ]
    for copy in copies:
        copy.start()
    return copies


def widen(copy, buf, wide):
    channels, lons = buf.shape[:2]
    pitch = wide.shape[0] // channels
    copy.wait()

    def body(c, carry):
        wide[pl.ds(pl.multiple_of(c * pitch, 8), lons), :] = buf[c].astype(F32)
        return carry

    lax.fori_loop(0, channels, body, 0, unroll=8)


def gate_rows(wide, lon, count, channels):
    pitch = wide.shape[0] // channels
    columns = [
        jnp.concatenate(
            [wide[pl.ds(c * pitch + r, 8, stride=pitch), :] for c in range(0, channels, 8)], axis=0
        )
        for r in range(lon, lon + count)
    ]
    return jnp.concatenate(columns, axis=1)


def inner_layers(low, inside, high, old, hid, gb, load, bufs, wide, wa, wb, near_out, finish, ends=None):
    cols = CHUNK * LANES
    step = DIL * LANES
    channels, total = hid.shape
    count = total // cols
    widen(load[0], bufs.at[0], wide)
    for i in range(count - 1):
        o = step + i * cols
        at = slice(o, o + cols)
        taps = [pieces(low, inside, high, o + d, cols) for d in (step, 0, -step)]
        back = conv(wa, taps)
        new = old(o, cols) + gate_rows(wide, o // LANES, CHUNK, channels) * back
        hid[:, at] = new
        gb[:, at] = new.astype(BF16)
    near_out[0] = hid[:, step : step + cols]
    near_out[1] = hid[:, total - step - cols : total - step]
    lons = total // LANES
    if ends is not None:
        ends[0] = gate_rows(wide, 0, DIL, channels).astype(BF16)
        ends[1] = gate_rows(wide, lons - DIL, DIL, channels).astype(BF16)
    widen(load[1], bufs.at[1], wide)
    for i in range(1, count - 1):
        o = i * cols
        at = slice(o, o + cols)
        back = conv(wb, [gb[:, o + d : o + d + cols] for d in (step, 0, -step)])
        finish(i, hid[:, at] + gate_rows(wide, o // LANES, CHUNK, channels) * back)


def mid_kernel(
    incr, key, group, hid_edge, g_lo, g_hi, dec, gates, w,
    grad_out, hid_out, field_out, near_out, ends_a, ends_b,
    hid, ga, gb, lhs, onehot, bufs, wide, sems,
):
    load = load_gates(gates, 3, bufs, sems)
    cols = CHUNK * LANES
    levels = incr.shape[0]
    channels, total = hid.shape
    inner = total // cols - 2
    onehot[...] = hot(key[...])
    for g in range(inner):
        mask = (group[0:1, :] == float(g + 1)).astype(F32).astype(BF16)
        lhs[g * levels : (g + 1) * levels, :] = incr[...] * mask
    hid[:, 0:cols] = hid_edge[0]
    hid[:, total - cols : total] = hid_edge[1]
    for n in range(0, cols, 256):
        grad_out[:, n : n + 256] = dot(lhs[...], onehot[:, n : n + 256])
    for g in range(inner):
        new = dot(dec[...], grad_out[g * levels : (g + 1) * levels, :].astype(BF16))
        hid[:, (g + 1) * cols : (g + 2) * cols] = new
        ga[:, g * cols : (g + 1) * cols] = new.astype(BF16)

    def old(o, size):
        return hid[:, o : o + size]

    def finish(i, value):
        hid_out[:, (i - 1) * cols : i * cols] = value
        field_out[:, (i - 1) * cols : i * cols] = value.astype(BF16)

    inner_layers(
        g_lo, ga, g_hi, old, hid, gb, load, bufs, wide, w.at[3], w.at[2], near_out, finish, ends_a
    )
    lons = total // LANES
    ends_b[0] = gate_rows(wide, 0, CHUNK, channels).astype(BF16)
    ends_b[1] = gate_rows(wide, lons - CHUNK, CHUNK, channels).astype(BF16)


def gates_scratch(gates):
    channels, lons, lats = gates.shape[1:]
    return [
        pltpu.VMEM((2, channels, lons, lats), BF16),
        pltpu.VMEM((channels * (lons + 8), lats), F32),
        pltpu.SemaphoreType.DMA((2,)),
    ]


def mid(incr, key, group, hid_edge, g_lo, g_hi, dec, gates, w):
    levels, slots = incr.shape
    channels, lons, lats = gates.shape[1:]
    total = lons * lats
    cols = CHUNK * LANES
    inner = total // cols - 2
    sd = jax.ShapeDtypeStruct
    outs = (
        sd((inner * levels, cols), F32),
        sd((channels, inner * cols), F32),
        sd((channels, inner * cols), BF16),
        sd((2, channels, cols), F32),
        sd((2, channels, DIL * LANES), BF16),
        sd((2, channels, cols), BF16),
    )
    return pl.pallas_call(
        mid_kernel,
        in_specs=[VMEM] * 7 + [HBM, VMEM],
        out_specs=(VMEM,) * 6,
        out_shape=outs,
        scratch_shapes=[
            pltpu.VMEM((channels, total), F32),
            pltpu.VMEM((channels, inner * cols), BF16),
            pltpu.VMEM((channels, total), BF16),
            pltpu.VMEM((inner * levels, slots), BF16),
            pltpu.VMEM((slots, cols), BF16),
        ]
        + gates_scratch(gates),
        compiler_params=params(40),
        name="mid",
    )(incr, key, group, hid_edge, g_lo, g_hi, dec, gates, w)


def emit(enc, grad, value, tile):
    full = grad + dot(enc, value.astype(BF16))
    for r in range(CHUNK):
        for l in range(0, full.shape[0], 8):
            tile[pl.ds(l * CHUNK + r, 8, stride=CHUNK), :] = full[
                l : l + 8, r * LANES : (r + 1) * LANES
            ]


def send_tile(tile, out, chunk, sem):
    levels = out.shape[0]
    src = tile.reshape(tile.shape[0] // CHUNK, CHUNK, LANES)
    return pltpu.make_async_copy(
        src.at[0:levels], out.at[:, CHUNK * chunk : CHUNK * (chunk + 1), :], sem
    )


def last_kernel(
    hid_in, field_in, hid_edge, g_lo, g_hi, grad, enc, gates, w,
    out, near_out, ends_a, ends_b, hid, gb, tiles, sems, bufs, wide, gate_sems,
):
    load = load_gates(gates, 1, bufs, gate_sems)
    channels, total = hid.shape
    levels = enc.shape[0]
    copies = []

    def old(o, size):
        return pieces(hid_edge.at[0], hid_in, hid_edge.at[1], o, size)

    def finish(i, value):
        slot = (i - 1) % 2
        if i > 2:
            copies[i - 3].wait()
        emit(enc[...], grad[(i - 1) * levels : i * levels, :], value, tiles.at[slot])
        copy = send_tile(tiles.at[slot], out, i, sems.at[slot])
        copy.start()
        copies.append(copy)

    inner_layers(
        g_lo, field_in, g_hi, old, hid, gb, load, bufs, wide, w.at[1], w.at[0], near_out, finish, ends_a
    )
    lons = total // LANES
    ends_b[0] = gate_rows(wide, 0, CHUNK, channels).astype(BF16)
    ends_b[1] = gate_rows(wide, lons - CHUNK, CHUNK, channels).astype(BF16)
    copies[-2].wait()
    copies[-1].wait()


def last(hid_in, field_in, hid_edge, g_lo, g_hi, grad, enc, gates, w, out_shape):
    channels, lons, lats = gates.shape[1:]
    total = lons * lats
    cols = CHUNK * LANES
    levels = enc.shape[0]
    sd = jax.ShapeDtypeStruct
    return pl.pallas_call(
        last_kernel,
        in_specs=[VMEM] * 7 + [HBM, VMEM],
        out_specs=(HBM, VMEM, VMEM, VMEM),
        out_shape=(
            sd(out_shape, F32),
            sd((2, channels, cols), F32),
            sd((2, channels, DIL * LANES), BF16),
            sd((2, channels, cols), BF16),
        ),
        scratch_shapes=[
            pltpu.VMEM((channels, total), F32),
            pltpu.VMEM((channels, total), BF16),
            pltpu.VMEM((2, levels * CHUNK, LANES), F32),
            pltpu.SemaphoreType.DMA((2,)),
        ]
        + gates_scratch(gates),
        compiler_params=params(40),
        name="last",
    )(hid_in, field_in, hid_edge, g_lo, g_hi, grad, enc, gates, w)


def edge_value(which, side, hid, g_lo, g_hi, halo, near, gate_a, gate_b, gate_halo, w):
    cols = CHUNK * LANES
    step = DIL * LANES
    wa, wb = w.at[2 * which + 1], w.at[2 * which]
    if side == 0:
        field = jnp.concatenate([halo[...], g_lo[...]], axis=1)
        old = jnp.concatenate([halo[:, step:].astype(F32), hid[0, :, :step]], axis=1)
        gate = jnp.concatenate([gate_halo[which], gate_a[0]], axis=1)
    else:
        field = jnp.concatenate([g_hi[...], halo[...]], axis=1)
        old = jnp.concatenate([hid[1, :, step:], halo[:, :step].astype(F32)], axis=1)
        gate = jnp.concatenate([gate_a[1], gate_halo[which]], axis=1)
    back = conv(wa, [field[:, d : d + cols] for d in (2 * step, step, 0)])
    new = old + gate.astype(F32) * back
    joined = jnp.concatenate((new, near[0]) if side == 0 else (near[1], new), axis=1)
    field = joined.astype(BF16)
    back = conv(wb, [field[:, d : d + cols] for d in (2 * step, step, 0)])
    return joined[:, step : step + cols] + gate_b[side].astype(F32) * back


def edge_far_kernel(which, odd, *refs):
    ins, (hid_out, send) = refs[:9], refs[9:]

    def body(side):
        value = edge_value(which, side, *ins)
        hid_out[...] = value
        send[...] = value.astype(BF16)

    by_side(odd, True, body)


def edge_close_kernel(which, odd, *refs):
    ins, (far_hid, far_g), (hid_out, lo_out, hi_out, send) = refs[:9], refs[9:11], refs[11:]

    def body(side):
        value = edge_value(which, side, *ins)
        hid_out[side] = value
        send[...] = value.astype(BF16)
        (lo_out, hi_out)[side][...] = value.astype(BF16)
        hid_out[1 - side] = far_hid[...]
        (hi_out, lo_out)[side][...] = far_g[...]

    by_side(odd, False, body)


def edge_last_kernel(which, odd, hid, g_lo, g_hi, far, close, near, gate_a, gate_b, far_gate, close_gate, w, grad, enc, state, out, tiles, sems):
    del state
    levels = enc.shape[0]
    chunks = out.shape[1] // CHUNK

    def body(far_side):
        values = []
        for side in range(2):
            halo, gate = (far, far_gate) if side == far_side else (close, close_gate)
            values.append(
                edge_value(which, side, hid, g_lo, g_hi, halo, near, gate_a, gate_b, gate, w)
            )
        copies = []
        for side in range(2):
            part = grad[side * levels : (side + 1) * levels, :]
            emit(enc[...], part, values[side], tiles.at[side])
            copy = send_tile(tiles.at[side], out, side * (chunks - 1), sems.at[side])
            copy.start()
            copies.append(copy)
        for copy in copies:
            copy.wait()

    by_side(odd, True, body)


def edge_far(which, *args):
    sd = jax.ShapeDtypeStruct
    g_lo = args[2]
    return pl.pallas_call(
        functools.partial(edge_far_kernel, which),
        in_specs=[SMEM] + [VMEM] * 9,
        out_specs=(VMEM,) * 2,
        out_shape=(sd(g_lo.shape, F32), sd(g_lo.shape, BF16)),
        compiler_params=params(18),
        name="edge_far",
    )(*args)


def edge_close(which, *args):
    sd = jax.ShapeDtypeStruct
    hid, g_lo = args[1:3]
    return pl.pallas_call(
        functools.partial(edge_close_kernel, which),
        in_specs=[SMEM] + [VMEM] * 11,
        out_specs=(VMEM,) * 4,
        out_shape=(sd(hid.shape, F32),) + (sd(g_lo.shape, BF16),) * 3,
        compiler_params=params(18),
        name="edge_close",
    )(*args)


def edge_last(which, *args):
    enc, state = args[-2:]
    return pl.pallas_call(
        functools.partial(edge_last_kernel, which),
        in_specs=[SMEM] + [VMEM] * 13 + [HBM],
        out_specs=HBM,
        out_shape=jax.ShapeDtypeStruct(state.shape, F32),
        scratch_shapes=[
            pltpu.VMEM((2, enc.shape[0] * CHUNK, LANES), F32),
            pltpu.SemaphoreType.DMA((2,)),
        ],
        input_output_aliases={14: 0},
        compiler_params=params(18),
        name="edge_last",
    )(*args)


def swap(value, first):
    count = lax.axis_size("lon")
    pairs = []
    for i in range(first, first + count, 2):
        low, high = i % count, (i + 1) % count
        pairs += [(low, high), (high, low)]
    return lax.ppermute(value, "lon", pairs)


def program(resid, index, count, weight, jacobian, decoder, conv_weight, gates, encoder):
    dests = lax.axis_size("lat") * lax.axis_size("lon")
    odd = (lax.axis_index("lon") % 2).astype(jnp.int32).reshape(1)
    packed = pack(resid, index, count, weight.reshape(1, -1), dests)
    packed = lax.all_to_all(packed, ("lat", "lon"), split_axis=0, concat_axis=0, tiled=True)
    gate_far, gate_close = gate_edges(odd, gates)
    gate_far_halo = swap(gate_far, 1)
    gate_close_halo = swap(gate_close, 0)
    jac, dec, enc, w = prepare(jacobian, decoder, encoder, conv_weight, gate_far)
    incr, key, group, grad_e, hid_e, g_lo, g_hi, far, close = front(odd, packed, jac, dec)
    far = swap(far, 1)
    close = swap(close, 0)
    grad_i, hid_i, field_i, near, end_a, end_b = mid(
        incr, key, group, hid_e, g_lo, g_hi, dec, gates, w
    )
    far_hid, far_g = edge_far(1, odd, hid_e, g_lo, g_hi, far, near, end_a, end_b, gate_far_halo, w)
    far = swap(far_g, 1)
    hid_e, g_lo, g_hi, close = edge_close(
        1, odd, hid_e, g_lo, g_hi, close, near, end_a, end_b, gate_close_halo, w, far_hid, far_g
    )
    close = swap(close, 0)
    out_shape = (jacobian.shape[2],) + gates.shape[2:]
    state, near, end_a, end_b = last(
        hid_i, field_i, hid_e, g_lo, g_hi, grad_i, enc, gates, w, out_shape
    )
    return edge_last(
        0, odd, hid_e, g_lo, g_hi, far, close, near, end_a, end_b,
        gate_far_halo, gate_close_halo, w, grad_e, enc, state,
    )


def solution(mesh):
    return jax.shard_map(
        program,
        mesh=mesh,
        in_specs=(
            P(None, ("lat", "lon")),
            P(None, ("lat", "lon")),
            P(None, ("lat", "lon")),
            P(),
            P(),
            P(),
            P(),
            P(None, None, "lon", "lat"),
            P(),
        ),
        out_specs=P(None, "lon", "lat"),
        check_vma=False,
    )
```
